512 devices in a mesh: sub: 128 (over y, z, core), case: 4 (over x).
Axes of the slice: x: 4, y: 8, z: 8, core: 2. Of those that a mesh axis runs over, the one named last changes fastest.
Arguments:
- multipliers: float32 [64, 196608], P('case', 'sub'), may hold values from -6 to 6
- right_side: float32 [64, 196608], P('case', 'sub')
- dual_ops: bfloat16 [196608, 1536], P('sub'), as said below
- glue_match: int32 [128, 2, 128], P('sub'), may hold values from 0 to 127, as said below
- mortar: bfloat16 [128, 4, 128, 128], P('sub'), may hold values from -0.5 to 0.5
- contact_ids: int32 [128, 4], P('sub'), may hold values from 0 to 3
- contact_count: int32 [128], P('sub'), may hold values from 1 to 4
Outputs:
- solved: float32 [64, 196608], P('case', 'sub')
- grad_norm: float32 [1], replicated
The draws below stay inside these ranges and needn't reach their ends.
Inputs may be any that keep to these rules, and one draw needn't show every extreme that they name: glue_match[s,1] is a permutation of 0 to 127, and glue_match[(s+1) mod 128,0] is its inverse. `dual_ops`: each subdomain's block is symmetric positive definite.
All inputs are finite; a program needn't handle non-finite values.
Results may differ from the reference program's by a relative error of at most 0.002.
Values may be sent and summed in bfloat16 or wider, within the bound.
No kernel may reach another device: no remote copies, remote signals or barrier semaphores. Data moves between devices by JAX's collectives and lax.ppermute only.
A program may use at most 64 MiB of HBM per device.

```python
import jax
import jax.numpy as jnp
from jax import lax

M = 1536
BLK = 128
C = 64
ITERS = 4
SUBS = 128
N_SUB = 128


def draw_dual_ops(key, part):
    key_noise = jax.random.fold_in(key, 11)
    key_diag = jax.random.fold_in(key, 12)
    noise = jax.random.normal(key_noise, (SUBS, M, M), jnp.float32)
    symmetric = (noise + jnp.swapaxes(noise, 1, 2)) * (0.35 / jnp.sqrt(2.0 * M))
    diagonal = jax.random.uniform(key_diag, (SUBS, M), jnp.float32, 1.0, 2.0)
    operators = symmetric + diagonal[:, :, None] * jnp.eye(M, dtype=jnp.float32)[None]
    return operators.reshape(SUBS * M, M).astype(jnp.bfloat16)


def draw_right_side(key, part):
    key_base = jax.random.fold_in(key, 31)
    key_rough = jax.random.fold_in(key, 32)
    base = jax.random.normal(key_base, (C, SUBS, M), jnp.float32)
    sub_rise = 4.0 ** (jnp.arange(SUBS, dtype=jnp.float32) / (SUBS - 1))
    case_rise = 3.0 ** (jnp.arange(C, dtype=jnp.float32) / (C - 1))
    rough = jax.random.uniform(key_rough, (SUBS, M), jnp.float32, 0.5, 1.5)
    values = base * sub_rise[None, :, None] * rough[None] * case_rise[:, None, None]
    return values.reshape(C, SUBS * M)


def draw_glue_match(key, part):
    keys = jax.random.split(jax.random.fold_in(key, 21), SUBS)
    perms = jax.vmap(lambda single: jax.random.permutation(single, BLK))(keys).astype(jnp.int32)
    inverse = jnp.argsort(perms, axis=1).astype(jnp.int32)
    first = jnp.roll(inverse, 1, axis=0)
    return jnp.stack([first, perms], axis=1)


def draw_contact_count(key, part):
    key_counts = jax.random.fold_in(key, 41)
    key_full = jax.random.fold_in(key, 42)
    key_low = jax.random.fold_in(key, 43)
    counts = jax.random.randint(key_counts, (SUBS,), 1, 5)
    full_at = jax.random.randint(key_full, (), 0, SUBS)
    low_at = (full_at + 1 + jax.random.randint(key_low, (), 0, SUBS - 1)) % SUBS
    counts = counts.at[full_at].set(4).at[low_at].set(1)
    return counts.astype(jnp.int32)


def set_ends(result, stream_key, smallest, top_value):
    place = [jax.random.randint(jax.random.fold_in(stream_key, axis), (), 0, length) for axis, length in enumerate(result.shape)]
    longest = result.shape.index(max(result.shape))
    beside = place[:longest] + [(place[longest] + 1) % result.shape[longest]] + place[longest + 1:]
    return result.at[tuple(place)].set(smallest).at[tuple(beside)].set(top_value)


def level_of(rng, shape, cuts, low, high):
    def one(position, blocks):
        steps = jax.random.uniform(jax.random.fold_in(jax.random.fold_in(rng, 6), position), (blocks,), jnp.float32, low / len(cuts), high / len(cuts))
        return jnp.repeat(jnp.exp(steps), shape[position] // blocks).reshape((-1,) + (1,) * (len(shape) - position - 1))

    gain = one(*cuts[0])
    for cut in cuts[1:]:
        gain = gain * one(*cut)
    return gain


def centred(stream_key, shape, deviation, reach, cuts=(), kind=jnp.bfloat16):
    values = deviation * jax.random.normal(stream_key, shape, jnp.float32)
    if cuts:
        values = values * level_of(stream_key, shape, cuts, -0.22, 0.18)
    return jnp.clip(values, -reach, reach).astype(kind)


def setup_inputs(seed: int = 0) -> dict:
    arg_keys = jax.random.split(jax.random.key(seed), 8)
    return {
        "multipliers": centred(arg_keys[0], (C, SUBS * M), 1.0, 6.0, ((0, 4), (1, 128)), jnp.float32),
        "right_side": draw_right_side(jax.random.fold_in(arg_keys[7], 71), 0),
        "dual_ops": draw_dual_ops(jax.random.fold_in(arg_keys[7], 71), 0),
        "glue_match": draw_glue_match(jax.random.fold_in(arg_keys[7], 71), 0),
        "mortar": centred(arg_keys[4], (SUBS, 4, BLK, BLK), BLK ** -0.5, 0.5, ((0, 128),)),
        "contact_ids": set_ends(jax.random.randint(arg_keys[5], (SUBS, 4), 0, 4), jax.random.fold_in(arg_keys[5], 1), 0, 3).astype(jnp.int32),
        "contact_count": draw_contact_count(jax.random.fold_in(arg_keys[7], 71), 0),
    }


penalty = 0.5
exact_mode = lax.Precision.HIGHEST

def apply_operator(vector, dual_ops, glue_match, mortar, contact_ids, contact_count):
    case_cols = vector.shape[0]
    pieces = jnp.swapaxes(vector.astype(jnp.bfloat16).reshape(case_cols, N_SUB, M), 0, 1)
    operators = dual_ops.reshape(N_SUB, M, M)

    def one_product(pair):
        return jnp.dot(pair[0], pair[1], preferred_element_type=jnp.float32)
    local_part = jnp.swapaxes(lax.map(one_product, (pieces, operators)), 0, 1)
    mortar_f = mortar.astype(jnp.float32)
    blocks = vector.reshape(case_cols, N_SUB, 12, BLK)
    prev_face = jnp.roll(blocks[:, :, 1, :], 1, axis=1)
    next_face = jnp.roll(blocks[:, :, 0, :], -1, axis=1)
    first_index = jnp.broadcast_to(glue_match[None, :, 0, :], (case_cols, N_SUB, BLK))
    second_index = jnp.broadcast_to(glue_match[None, :, 1, :], (case_cols, N_SUB, BLK))
    swapped_first = jnp.take_along_axis(prev_face, first_index, axis=2)
    swapped_second = jnp.take_along_axis(next_face, second_index, axis=2)
    face_part = penalty * (blocks[:, :, 0:2, :] - jnp.stack([swapped_first, swapped_second], axis=2))
    own_blocks = blocks[:, :, 2:6, :]
    slave_blocks = jnp.roll(own_blocks, N_SUB // 2, axis=1)
    onehot = (contact_ids[:, :, None] == jnp.arange(4, dtype=jnp.int32)[None, None, :]).astype(jnp.float32)
    selected = jnp.einsum('nkb,cnbe->cnke', onehot, slave_blocks, precision=exact_mode)
    active = (jnp.arange(4, dtype=jnp.int32)[None, :] < contact_count[:, None]).astype(jnp.float32)
    mortar_jump = (jnp.einsum('cnke,nkef->cnkf', selected, mortar_f, precision=exact_mode) - own_blocks) * active[None, :, :, None]
    reply_rows = jnp.einsum('cnkf,nkef->cnke', mortar_jump, mortar_f, precision=exact_mode)
    back_rows = jnp.einsum('nkb,cnke->cnbe', onehot, reply_rows, precision=exact_mode)
    returned = jnp.roll(back_rows, N_SUB // 2, axis=1)
    correction = jnp.concatenate([face_part, returned - mortar_jump, jnp.zeros((case_cols, N_SUB, 6, BLK), jnp.float32)], axis=2)
    return local_part.reshape(case_cols, N_SUB * M) + correction.reshape(case_cols, N_SUB * M)

def reference(multipliers, right_side, dual_ops, glue_match, mortar, contact_ids, contact_count):
    current = multipliers
    grad_norms = jnp.zeros((multipliers.shape[0],), jnp.float32)
    for iteration in range(ITERS):
        gradient = apply_operator(current, dual_ops, glue_match, mortar, contact_ids, contact_count) - right_side
        grad_norms = lax.optimization_barrier(jnp.sum(gradient * gradient, axis=1))
        curved = apply_operator(gradient, dual_ops, glue_match, mortar, contact_ids, contact_count)
        grad_curves = lax.optimization_barrier(jnp.sum(gradient * curved, axis=1))
        step_size = grad_norms / grad_curves
        moved = current - step_size[:, None] * gradient
        moved_blocks = moved.reshape(moved.shape[0], N_SUB, 12, BLK)
        clipped = jnp.concatenate([moved_blocks[:, :, 0:2], jnp.maximum(moved_blocks[:, :, 2:6], 0.0), moved_blocks[:, :, 6:12]], axis=2)
        current = clipped.reshape(moved.shape)
    return (current, jnp.sqrt(jnp.sum(grad_norms)).reshape(1))
```

```python
import jax
import jax.numpy as jnp
from jax import lax
from jax.sharding import PartitionSpec as P

M = 1536
BLK = 128
ITERS = 4
CASES = 16

penalty = 0.5


def shifted(value, axis, by):
    devices = lax.axis_size(axis)
    return lax.ppermute(value, axis, [(i, (i + by) % devices) for i in range(devices)])


def two_parts(value):
    high = value.astype(jnp.bfloat16)
    low = (value - high.astype(jnp.float32)).astype(jnp.bfloat16)
    return jnp.concatenate([high, low], axis=-2)


def joined(product):
    rows = product.shape[-2] // 2
    return product[..., :rows, :] + product[..., rows:, :]


def times(value, matrix):
    return joined(jnp.matmul(two_parts(value), matrix, preferred_element_type=jnp.float32))


def times_transposed(value, matrix):
    return joined(
        jnp.einsum("kcf,kef->kce", two_parts(value), matrix, preferred_element_type=jnp.float32)
    )


def blocks_of(rows):
    return jnp.stack([rows[:, k * BLK : (k + 1) * BLK] for k in range(rows.shape[1] // BLK)])


def jump_of(slave, own, onehot, active, mortar):
    selected = jnp.einsum("kb,bce->kce", onehot, slave, precision=lax.Precision.HIGHEST)
    return (times(selected, mortar) - own) * active[:, None, None]


def reply_of(jump, onehot, mortar):
    rows = times_transposed(jump, mortar)
    return jnp.einsum("kb,kce->bce", onehot, rows, precision=lax.Precision.HIGHEST)


def slot_terms(ids, count):
    onehot = (ids[:, None] == jnp.arange(4, dtype=ids.dtype)[None, :]).astype(jnp.float32)
    active = (jnp.arange(4, dtype=count.dtype) < count).astype(jnp.float32)
    return onehot, active


def summed_over(value, axis):
    devices = lax.axis_size(axis)
    copies = jnp.broadcast_to(value[None], (devices,) + value.shape)
    return lax.all_to_all(copies, axis, 0, 0).sum(0)


def on_device(multipliers, right_side, dual_ops, glue_match, mortar, contact_ids, contact_count):
    half_axis = lax.axis_size("sub") // 2
    mortar = mortar[0]
    onehot, active = slot_terms(contact_ids[0], contact_count[0])

    meta = jnp.concatenate([contact_ids[0], contact_count]).astype(jnp.bfloat16)
    meta = jnp.zeros((16, BLK), jnp.bfloat16).at[0, :5].set(meta)
    contact = multipliers[:, 2 * BLK : 6 * BLK]
    packed = jnp.concatenate(
        [
            blocks_of(contact).astype(jnp.bfloat16).reshape(4 * CASES, BLK),
            mortar.reshape(4 * BLK, BLK),
            meta,
        ]
    )
    packed = shifted(packed, "sub", half_axis)
    mate = packed[: 4 * CASES].astype(jnp.float32).reshape(4, CASES, BLK)
    mate_mortar = packed[4 * CASES : 4 * CASES + 4 * BLK].reshape(4, BLK, BLK)
    mate_meta = packed[4 * CASES + 4 * BLK].astype(jnp.int32)
    mate_onehot, mate_active = slot_terms(mate_meta[:4], mate_meta[4])

    lanes = jnp.arange(BLK, dtype=jnp.int32)
    pick = (lanes[None, :, None] == glue_match[0][:, None, :]).astype(jnp.bfloat16)

    x = multipliers
    prev_x = shifted(multipliers[:, BLK : 2 * BLK], "sub", 1)
    next_x = shifted(multipliers[:, :BLK], "sub", -1)
    total_norm = None
    for iteration in range(ITERS):
        local = jnp.dot(x.astype(jnp.bfloat16), dual_ops, preferred_element_type=jnp.float32)
        faces = [x[:, :BLK] - times(prev_x, pick[0]), x[:, BLK : 2 * BLK] - times(next_x, pick[1])]
        own = blocks_of(x[:, 2 * BLK : 6 * BLK])
        jump = jump_of(mate, own, onehot, active, mortar)
        mate_jump = jump_of(own, mate, mate_onehot, mate_active, mate_mortar)
        part = reply_of(mate_jump, mate_onehot, mate_mortar) - jump
        correction = jnp.concatenate(
            [penalty * face for face in faces]
            + [part[k] for k in range(4)]
            + [jnp.zeros((CASES, 6 * BLK), jnp.float32)],
            axis=1,
        )
        gradient = local + correction - right_side

        own_g = blocks_of(gradient[:, 2 * BLK : 6 * BLK])
        mate_g = shifted(own_g.astype(jnp.bfloat16), "sub", half_axis).astype(jnp.float32)
        prev_g = shifted(gradient[:, BLK : 2 * BLK], "sub", 1)
        next_g = shifted(gradient[:, :BLK], "sub", -1)
        image = jnp.dot(
            gradient.astype(jnp.bfloat16), dual_ops, preferred_element_type=jnp.float32
        )
        first, second = gradient[:, :BLK], gradient[:, BLK : 2 * BLK]
        jump = jump_of(mate_g, own_g, onehot, active, mortar)
        face_curve = penalty * (first * first + second * second) - first * times(prev_g, pick[0])
        curve = (
            jnp.sum(gradient * image, axis=1)
            + jnp.sum(face_curve, axis=1)
            + jnp.sum(jump * jump, axis=(0, 2))
        )
        norm = jnp.sum(gradient * gradient, axis=1)
        both = jnp.concatenate([norm, curve, jnp.zeros((BLK - 2 * CASES,), jnp.float32)])
        both = summed_over(both.reshape(1, BLK), "sub")[0]
        norm, curve = both[:CASES], both[CASES : 2 * CASES]
        step = (norm / curve)[:, None]
        moved = x - step * gradient
        x = jnp.concatenate(
            [
                moved[:, : 2 * BLK],
                jnp.maximum(moved[:, 2 * BLK : 6 * BLK], 0.0),
                moved[:, 6 * BLK :],
            ],
            axis=1,
        )
        if iteration < ITERS - 1:
            mate = jnp.maximum(mate - step[None] * mate_g, 0.0)
            prev_x = prev_x - step * prev_g
            next_x = next_x - step * next_g
    total_norm = summed_over(jnp.full((1, BLK), jnp.sum(norm), jnp.float32), "case")
    return (x, jnp.sqrt(total_norm[0, :1]))


def solution(mesh):
    in_specs = (
        P("case", "sub"),
        P("case", "sub"),
        P("sub", None),
        P("sub", None, None),
        P("sub", None, None, None),
        P("sub", None),
        P("sub"),
    )
    out_specs = (P("case", "sub"), P())
    return jax.shard_map(
        on_device, mesh=mesh, in_specs=in_specs, out_specs=out_specs, check_vma=False
    )
```

```python
import jax
import jax.numpy as jnp
from jax import lax
from jax.experimental import pallas as pl
from jax.experimental.pallas import tpu as pltpu
from jax.sharding import PartitionSpec as P

M = 1536
BLK = 128
ITERS = 4
CASES = 16
LOW, HIGH = 2 * BLK, 6 * BLK
CONTACT = HIGH - LOW

penalty = 0.5
f32, bf16 = jnp.float32, jnp.bfloat16


def dot(value, matrix, transposed=False):
    contract = 1 if transposed else 0
    return lax.dot_general(
        value, matrix, (((1,), (contract,)), ((), ())), preferred_element_type=f32
    )


def fine_dot(value, matrix, transposed=False):
    high = value.astype(bf16)
    low = (value - high.astype(f32)).astype(bf16)
    both = dot(jnp.concatenate([high, low], axis=0), matrix, transposed)
    return both[:CASES] + both[CASES:]


def split(value):
    return [value[:, k * BLK : (k + 1) * BLK] for k in range(value.shape[1] // BLK)]


def weighed(weights, values):
    total = weights[0] * values[0]
    for weight, value in zip(weights[1:], values[1:]):
        total = total + weight * value
    return total


def slots(meta):
    onehot = [[meta[:, 4 * k + b : 4 * k + b + 1] for b in range(4)] for k in range(4)]
    active = [meta[:, 16 + k : 17 + k] for k in range(4)]
    return onehot, active


def slot_table(ids, count):
    lane = lax.broadcasted_iota(jnp.int32, (CASES, BLK), 1)
    table = jnp.zeros((CASES, BLK), f32)
    for k in range(4):
        table = jnp.where(lane == ids[0, k] + 4 * k, 1.0, table)
        alive = jnp.where(count[0] > k, 1.0, 0.0).astype(f32)
        table = jnp.where(lane == 16 + k, alive, table)
    return table


def jump_of(slave, own, terms, mortar):
    onehot, active = terms
    return [
        (fine_dot(weighed(onehot[k], slave), mortar[k]) - own[k]) * active[k] for k in range(4)
    ]


def reply_of(jump, terms, mortar):
    onehot, _ = terms
    rows = [fine_dot(jump[k], mortar[k], True) for k in range(4)]
    return [weighed([onehot[k][b] for k in range(4)], rows) for b in range(4)]


def contact_terms(own, mate, statics, both):
    terms, mortar, mate_terms, mate_mortar = statics[:4]
    own, mate = split(own), split(mate)
    jump = jump_of(mate, own, terms, mortar)
    mate_jump = jump_of(own, mate, mate_terms, mate_mortar)
    part = [r - j for r, j in zip(reply_of(mate_jump, mate_terms, mate_mortar), jump)]
    if not both:
        return jnp.concatenate(part, axis=1), None
    mate_part = [r - j for r, j in zip(reply_of(jump, terms, mortar), mate_jump)]
    return jnp.concatenate(part, axis=1), jnp.concatenate(mate_part, axis=1)


def picks(match):
    rows = lax.broadcasted_iota(jnp.int32, (BLK, BLK), 0)
    return [
        jnp.where(rows == match[side : side + 1, :], 1.0, 0.0).astype(bf16) for side in range(2)
    ]


def whole_dot(value, pieces):
    high = value.astype(bf16)
    low = (value - high.astype(f32)).astype(bf16)
    both, total = jnp.concatenate([high, low], axis=0), None
    for start, size, piece in pieces:
        part = dot(both[:, start : start + size], piece())
        total = part if total is None else total + part
    return total[:CASES] + total[CASES:]


def begin(x, q, mate, prev, following, statics):
    pick = statics[4]
    mate_x, mate_q = mate[:, :CONTACT], mate[:, CONTACT:]
    prev_x, prev_q, prev_contact = prev[:, :BLK], prev[:, BLK : 2 * BLK], prev[:, 2 * BLK :]
    next_x, next_q = following[:, :BLK], following[:, BLK : 2 * BLK]
    next_contact = following[:, 2 * BLK :]
    first, second = x[:, :BLK], x[:, BLK:LOW]
    part, mate_part = contact_terms(x[:, LOW:HIGH], mate_x, statics, True)
    g = jnp.concatenate(
        [
            q[:, :BLK] + penalty * (first - fine_dot(prev_x, pick[0])),
            q[:, BLK:LOW] + penalty * (second - fine_dot(next_x, pick[1])),
            q[:, LOW:HIGH] + part,
            q[:, HIGH:],
        ],
        axis=1,
    )
    mate_g = mate_q + mate_part
    prev_face = prev_q + penalty * (prev_x - fine_dot(first, pick[0], True))
    next_face = next_q + penalty * (next_x - fine_dot(second, pick[1], True))
    others = jnp.concatenate([mate_x, mate_g, prev_contact, next_contact], axis=1)
    return g, others, prev_face, next_face


def tail(g, mate_g, prev_face, next_face, statics, pieces):
    pick = statics[4]
    part, _ = contact_terms(g[:, LOW:HIGH], mate_g, statics, False)
    first = penalty * (g[:, :BLK] - fine_dot(prev_face, pick[0]))
    second = penalty * (g[:, BLK:LOW] - fine_dot(next_face, pick[1]))
    zeros = jnp.zeros((CASES, M - HIGH), f32)
    image = whole_dot(g, pieces)
    image = image + jnp.concatenate([first, second, part, zeros], axis=1)
    norm = jnp.sum(g * g, axis=1, keepdims=True)
    curve = jnp.sum(g * image, axis=1, keepdims=True)
    lane = lax.broadcasted_iota(jnp.int32, (CASES, BLK), 1)
    row = lax.broadcasted_iota(jnp.int32, (CASES, BLK), 0)
    spread = jnp.where(lane == row, norm, 0.0) + jnp.where(lane == row + CASES, curve, 0.0)
    return image, jnp.sum(spread, axis=0, keepdims=True)


def step_of(sums):
    total = jnp.sum(sums, axis=0, keepdims=True)
    lane = lax.broadcasted_iota(jnp.int32, (CASES, BLK), 1)
    row = lax.broadcasted_iota(jnp.int32, (CASES, BLK), 0)
    norm = jnp.sum(jnp.where(lane == row, total, 0.0), axis=1, keepdims=True)
    curve = jnp.sum(jnp.where(lane == row + CASES, total, 0.0), axis=1, keepdims=True)
    return norm, norm / curve


def moved_by(x, step, g):
    moved = x - step * g
    return jnp.maximum(moved, 0.0), jnp.maximum(-moved, 0.0)


def all_moved(x, step, g):
    moved = x - step * g
    contact = moved[:, LOW:HIGH]
    x = jnp.concatenate([moved[:, :LOW], jnp.maximum(contact, 0.0), moved[:, HIGH:]], axis=1)
    return x, jnp.maximum(-contact, 0.0)


def advance(sums, own, others, mate, prev, following, statics, rows, coarse):
    _, step = step_of(sums)
    x, g, image = own
    x, lift = all_moved(x, step, g)
    mate_x, mate_g = others[:, :CONTACT], others[:, CONTACT : 2 * CONTACT]
    prev_x = others[:, 2 * CONTACT : 3 * CONTACT]
    next_x = others[:, 3 * CONTACT : 4 * CONTACT]
    prev_face = others[:, 4 * CONTACT : 4 * CONTACT + BLK]
    next_face = others[:, 4 * CONTACT + BLK :]
    mate_kernel, prev_kernel, next_kernel = coarse
    mate_x, mate_lift = moved_by(mate_x, step, mate_g)
    prev_x, prev_lift = moved_by(prev_x, step, prev[:, BLK:])
    next_x, next_lift = moved_by(next_x, step, following[:, BLK:])
    part, mate_part = contact_terms(lift, mate_lift, statics, True)
    mate_g = mate_g - step * mate + dot(mate_lift.astype(bf16), mate_kernel[...]) + mate_part
    prev_face = prev_face - step * prev[:, :BLK] + dot(prev_lift.astype(bf16), prev_kernel[...])
    next_face = next_face - step * following[:, :BLK] + dot(next_lift.astype(bf16), next_kernel[...])
    lifted = whole_dot(lift, [(start - LOW, size, piece) for start, size, piece in rows()])
    g = g - step * image + lifted
    g = jnp.concatenate([g[:, :LOW], g[:, LOW:HIGH] + part, g[:, HIGH:]], axis=1)
    others = jnp.concatenate([mate_x, mate_g, prev_x, next_x], axis=1)
    return x, g, others, prev_face, next_face


def to_partner(image):
    return image[:, LOW:HIGH]


def to_neighbour(image, g, side):
    face = image[:, side * BLK : (side + 1) * BLK]
    return jnp.concatenate([face, g[:, LOW:HIGH]], axis=1)


CHUNK = 256
STARTS = (LOW, LOW + CHUNK) + (0,) + tuple(range(HIGH, M, CHUNK))


def whole_copy(dual_hbm, dual_ref, sems):
    copies = []
    for index, start in enumerate(STARTS):
        rows = pl.ds(start, CHUNK)
        copies.append(
            pltpu.make_async_copy(dual_hbm.at[rows], dual_ref.at[rows], sems.at[index])
        )
    for copy in copies:
        copy.start()

    def piece(index, wait):
        def read():
            if wait:
                copies[index].wait()
            return dual_ref[pl.ds(STARTS[index], CHUNK), :]

        return (STARTS[index], CHUNK, read)

    return piece


def prepare_kernel(*refs):
    ids, count, x_ref, right_ref, mortar, dual_hbm = refs[:6]
    q_ref, packed, next_ref, prev_ref, dual_ref, sems = refs[6:]
    piece = whole_copy(dual_hbm, dual_ref, sems)
    packed[16 * CASES : 16 * CASES + CONTACT, :] = mortar[...]
    packed[16 * CASES + CONTACT :, :] = slot_table(ids, count).astype(bf16)
    x = x_ref[...]
    q = whole_dot(x, [piece(k, True) for k in range(len(STARTS))]) - right_ref[...]
    q_ref[...] = q
    for k, block in enumerate(split(x[:, LOW:HIGH]) + split(q[:, LOW:HIGH])):
        high = block.astype(bf16)
        packed[2 * k * CASES : (2 * k + 1) * CASES, :] = high
        low = (block - high.astype(f32)).astype(bf16)
        packed[(2 * k + 1) * CASES : (2 * k + 2) * CASES, :] = low
    next_ref[...] = jnp.concatenate([x[:, BLK:LOW], q[:, BLK:LOW], x[:, LOW:HIGH]], axis=1)
    prev_ref[...] = jnp.concatenate([x[:, :BLK], q[:, :BLK], x[:, LOW:HIGH]], axis=1)


def statics_of(ids, count, mortar, packed, match):
    start = 16 * CASES
    own = [mortar[k * BLK : (k + 1) * BLK, :] for k in range(4)]
    mate = [packed[start + k * BLK : start + (k + 1) * BLK, :] for k in range(4)]
    mate_table = packed[start + CONTACT :, :].astype(f32)
    return slots(slot_table(ids, count)), own, slots(mate_table), mate, picks(match[...])


def emit(outs, x, g, image, row, others, faces):
    own_out, others_out, row_out, mate_out, next_out, prev_out = outs
    row_out[...] = jnp.broadcast_to(row, row_out.shape)
    own_out[:, :M] = x
    own_out[:, M : 2 * M] = g
    own_out[:, 2 * M :] = image
    others_out[:, : 4 * CONTACT] = others
    others_out[:, 4 * CONTACT : 4 * CONTACT + BLK] = faces[0]
    others_out[:, 4 * CONTACT + BLK :] = faces[1]
    mate_out[...] = to_partner(image)
    next_out[...] = to_neighbour(image, g, 1)
    prev_out[...] = to_neighbour(image, g, 0)


def begin_kernel(*refs):
    ids, count, x_ref, q_ref, prev, following, mortar, packed, match, dual_hbm = refs[:10]
    outs, (dual_ref, sems) = refs[10:16], refs[16:]
    piece = whole_copy(dual_hbm, dual_ref, sems)
    statics = statics_of(ids, count, mortar, packed, match)
    x = x_ref[...]
    parts = [packed[k * CASES : (k + 1) * CASES, :].astype(f32) for k in range(16)]
    mate = jnp.concatenate([parts[2 * k] + parts[2 * k + 1] for k in range(8)], axis=1)
    g, others, prev_face, next_face = begin(
        x,
        q_ref[...],
        mate,
        prev[...],
        following[...],
        statics,
    )
    mate_g = others[:, CONTACT : 2 * CONTACT]
    pieces = [piece(k, True) for k in range(len(STARTS))]
    image, row = tail(g, mate_g, prev_face, next_face, statics, pieces)
    emit(outs, x, g, image, row, others, (prev_face, next_face))


def advance_kernel(*refs):
    ids, count, sums, own, others, mate, prev, following, mortar, packed, match = refs[:11]
    mate_kernel, prev_kernel, next_kernel, dual_hbm = refs[11:15]
    outs, (dual_ref, sems) = refs[15:21], refs[21:]
    piece = whole_copy(dual_hbm, dual_ref, sems)
    statics = statics_of(ids, count, mortar, packed, match)

    def rows():
        return [piece(k, True) for k in range(2)]

    x, g, others, prev_face, next_face = advance(
        sums[...],
        (own[:, :M], own[:, M : 2 * M], own[:, 2 * M :]),
        others[...],
        mate[...],
        prev[...],
        following[...],
        statics,
        rows,
        (mate_kernel, prev_kernel, next_kernel),
    )
    mate_g = others[:, CONTACT : 2 * CONTACT]
    pieces = [piece(k, k >= 2) for k in range(len(STARTS))]
    image, row = tail(g, mate_g, prev_face, next_face, statics, pieces)
    emit(outs, x, g, image, row, others, (prev_face, next_face))


def finish_kernel(sums, own, x_out, norm_out):
    norm, step = step_of(sums[...])
    x, _ = all_moved(own[:, :M], step, own[:, M : 2 * M])
    x_out[...] = x
    norm_out[...] = jnp.broadcast_to(jnp.sum(norm, axis=0, keepdims=True), norm_out.shape)


VMEM_SPEC = pl.BlockSpec(memory_space=pltpu.VMEM)
SMEM_SPEC = pl.BlockSpec(memory_space=pltpu.SMEM)
HBM_SPEC = pl.BlockSpec(memory_space=pltpu.HBM)


def call(kernel, specs, shapes, operands, scratch=True):
    scratch_shapes = [pltpu.VMEM((M, M), bf16), pltpu.SemaphoreType.DMA((len(STARTS),))] if scratch else []
    return pl.pallas_call(
        kernel,
        in_specs=specs,
        out_specs=[VMEM_SPEC] * len(shapes),
        out_shape=[jax.ShapeDtypeStruct(shape, kind) for shape, kind in shapes],
        scratch_shapes=scratch_shapes,
        compiler_params=pltpu.CompilerParams(vmem_limit_bytes=(52 if scratch else 16) << 20),
    )(*operands)


def shifted(value, by):
    devices = lax.axis_size("sub")
    return lax.ppermute(value, "sub", [(i, (i + by) % devices) for i in range(devices)])


def spread_sums(copies, axis):
    devices = lax.axis_size(axis)
    rows = lax.all_to_all(copies.reshape(devices, 1, BLK), axis, 0, 0)
    return rows.reshape(devices, BLK)


def on_device(multipliers, right_side, dual_ops, glue_match, mortar, contact_ids, contact_count):
    devices = lax.axis_size("sub")
    half_axis = devices // 2
    mortar = mortar.reshape(CONTACT, BLK)
    match = glue_match[0]
    scalars = [SMEM_SPEC, SMEM_SPEC]

    q, packed, following, prev = call(
        prepare_kernel,
        scalars + [VMEM_SPEC] * 3 + [HBM_SPEC],
        [
            ((CASES, M), f32),
            ((17 * CASES + CONTACT, BLK), bf16),
            ((CASES, 2 * BLK + CONTACT), f32),
            ((CASES, 2 * BLK + CONTACT), f32),
        ],
        (contact_ids, contact_count, multipliers, right_side, mortar, dual_ops),
    )
    packed = shifted(packed, half_axis)
    prev, following = shifted(following, 1), shifted(prev, -1)
    mate_kernel = shifted(dual_ops[LOW:HIGH, LOW:HIGH], half_axis)
    prev_kernel = shifted(dual_ops[LOW:HIGH, BLK:LOW], 1)
    next_kernel = shifted(dual_ops[LOW:HIGH, :BLK], -1)

    shapes = [
        ((CASES, 3 * M), f32),
        ((CASES, 4 * CONTACT + 2 * BLK), f32),
        ((devices, BLK), f32),
        ((CASES, CONTACT), f32),
        ((CASES, BLK + CONTACT), f32),
        ((CASES, BLK + CONTACT), f32),
    ]
    own, others, copies, to_mate, to_next, to_prev = call(
        begin_kernel,
        scalars + [VMEM_SPEC] * 7 + [HBM_SPEC],
        shapes,
        (
            contact_ids, contact_count, multipliers, q, prev, following, mortar, packed, match,
            dual_ops,
        ),
    )
    for _ in range(1, ITERS):
        sums = spread_sums(copies, "sub")
        mate = shifted(to_mate, half_axis)
        prev, following = shifted(to_next, 1), shifted(to_prev, -1)
        own, others, copies, to_mate, to_next, to_prev = call(
            advance_kernel,
            scalars + [VMEM_SPEC] * 12 + [HBM_SPEC],
            shapes,
            (
                contact_ids, contact_count, sums, own, others, mate, prev, following, mortar,
                packed, match, mate_kernel, prev_kernel, next_kernel, dual_ops,
            ),
        )
    sums = spread_sums(copies, "sub")
    x, norm = call(
        finish_kernel,
        [VMEM_SPEC, VMEM_SPEC],
        [((CASES, M), f32), ((lax.axis_size("case"), BLK), f32)],
        (sums, own),
        scratch=False,
    )
    total = spread_sums(norm, "case").sum(0)
    return (x, jnp.sqrt(total[:1]))


def solution(mesh):
    in_specs = (
        P("case", "sub"),
        P("case", "sub"),
        P("sub", None),
        P("sub", None, None),
        P("sub", None, None, None),
        P("sub", None),
        P("sub"),
    )
    out_specs = (P("case", "sub"), P())
    return jax.shard_map(
        on_device, mesh=mesh, in_specs=in_specs, out_specs=out_specs, check_vma=False
    )
```

```python
import jax
import jax.numpy as jnp
from jax import lax
from jax.experimental import pallas as pl
from jax.experimental.pallas import tpu as pltpu
from jax.sharding import PartitionSpec as P

M = 1536
BLK = 128
ITERS = 4
CASES = 16
LOW, HIGH = 2 * BLK, 6 * BLK
CONTACT = HIGH - LOW

penalty = 0.5
f32, bf16 = jnp.float32, jnp.bfloat16


def dot(value, matrix, transposed=False):
    contract = 1 if transposed else 0
    return lax.dot_general(
        value, matrix, (((1,), (contract,)), ((), ())), preferred_element_type=f32
    )


def fine_dot(value, matrix, transposed=False):
    high = value.astype(bf16)
    low = (value - high.astype(f32)).astype(bf16)
    both = dot(jnp.concatenate([high, low], axis=0), matrix, transposed)
    return both[:CASES] + both[CASES:]


def split(value):
    return [value[:, k * BLK : (k + 1) * BLK] for k in range(value.shape[1] // BLK)]


def weighed(weights, values):
    total = weights[0] * values[0]
    for weight, value in zip(weights[1:], values[1:]):
        total = total + weight * value
    return total


def slots(meta):
    onehot = [[meta[:, 4 * k + b : 4 * k + b + 1] for b in range(4)] for k in range(4)]
    active = [meta[:, 16 + k : 17 + k] for k in range(4)]
    return onehot, active


def slot_table(ids, count):
    lane = lax.broadcasted_iota(jnp.int32, (CASES, BLK), 1)
    table = jnp.zeros((CASES, BLK), f32)
    for k in range(4):
        table = jnp.where(lane == ids[0, k] + 4 * k, 1.0, table)
        alive = jnp.where(count[0] > k, 1.0, 0.0).astype(f32)
        table = jnp.where(lane == 16 + k, alive, table)
    return table


def jump_of(slave, own, terms, mortar):
    onehot, active = terms
    return [
        (fine_dot(weighed(onehot[k], slave), mortar[k]) - own[k]) * active[k] for k in range(4)
    ]


def reply_of(jump, terms, mortar):
    onehot, _ = terms
    rows = [fine_dot(jump[k], mortar[k], True) for k in range(4)]
    return [weighed([onehot[k][b] for k in range(4)], rows) for b in range(4)]


def contact_terms(own, mate, statics, both):
    terms, mortar, mate_terms, mate_mortar = statics[:4]
    own, mate = split(own), split(mate)
    jump = jump_of(mate, own, terms, mortar)
    mate_jump = jump_of(own, mate, mate_terms, mate_mortar)
    part = [r - j for r, j in zip(reply_of(mate_jump, mate_terms, mate_mortar), jump)]
    if not both:
        return jnp.concatenate(part, axis=1), None
    mate_part = [r - j for r, j in zip(reply_of(jump, terms, mortar), mate_jump)]
    return jnp.concatenate(part, axis=1), jnp.concatenate(mate_part, axis=1)


def chosen(even, first, second):
    return jnp.where(even, first, second)


def picks(match, even):
    rows = lax.broadcasted_iota(jnp.int32, (BLK, BLK), 0)
    first, second = match[0:1, :], match[1:2, :]
    sides = (chosen(even, second, first), chosen(even, first, second))
    return [jnp.where(rows == side, 1.0, 0.0).astype(bf16) for side in sides]


def faces_of(value, even):
    first, second = value[:, :BLK], value[:, BLK:LOW]
    return chosen(even, second, first), chosen(even, first, second)


def placed(near, far, even):
    return [chosen(even, far, near), chosen(even, near, far)]


def whole_dot(value, pieces):
    high = value.astype(bf16)
    low = (value - high.astype(f32)).astype(bf16)
    both, total = jnp.concatenate([high, low], axis=0), None
    for start, size, piece in pieces:
        part = dot(both[:, start : start + size], piece())
        total = part if total is None else total + part
    return total[:CASES] + total[CASES:]


def begin(x, q, mate, near, far, statics, pick, even):
    mate_x, mate_q = mate
    part, mate_part = contact_terms(x[:, LOW:HIGH], mate_x, statics, True)
    own = faces_of(x, even)
    glued, grads, contacts = [], [], []
    for side, face, matrix in zip((near, far), own, pick):
        side_x, side_q, contact = side[:, :BLK], side[:, BLK : 2 * BLK], side[:, 2 * BLK :]
        glued.append(penalty * (face - fine_dot(side_x, matrix)))
        grads.append(side_q + penalty * (side_x - fine_dot(face, matrix, True)))
        contacts.append(contact)
    faces = jnp.concatenate(placed(*glued, even), axis=1)
    g = jnp.concatenate(
        [q[:, :LOW] + faces, q[:, LOW:HIGH] + part, q[:, HIGH:]],
        axis=1,
    )
    return g, [mate_x, mate_q + mate_part] + contacts + grads


def tail(g, others, statics, pick, even, pieces):
    part, _ = contact_terms(g[:, LOW:HIGH], others[1], statics, False)
    glued = [
        penalty * (face - fine_dot(side, matrix))
        for face, side, matrix in zip(faces_of(g, even), others[4:], pick)
    ]
    zeros = jnp.zeros((CASES, M - HIGH), f32)
    image = whole_dot(g, pieces)
    image = image + jnp.concatenate(placed(*glued, even) + [part, zeros], axis=1)
    norm = jnp.sum(g * g, axis=1, keepdims=True)
    curve = jnp.sum(g * image, axis=1, keepdims=True)
    lane = lax.broadcasted_iota(jnp.int32, (CASES, BLK), 1)
    row = lax.broadcasted_iota(jnp.int32, (CASES, BLK), 0)
    spread = jnp.where(lane == row, norm, 0.0) + jnp.where(lane == row + CASES, curve, 0.0)
    return image, jnp.sum(spread, axis=0, keepdims=True)


def step_of(sums):
    total = jnp.sum(sums, axis=0, keepdims=True)
    lane = lax.broadcasted_iota(jnp.int32, (CASES, BLK), 1)
    row = lax.broadcasted_iota(jnp.int32, (CASES, BLK), 0)
    norm = jnp.sum(jnp.where(lane == row, total, 0.0), axis=1, keepdims=True)
    curve = jnp.sum(jnp.where(lane == row + CASES, total, 0.0), axis=1, keepdims=True)
    return norm, norm / curve


def moved_by(x, step, g):
    moved = x - step * g
    return jnp.maximum(moved, 0.0), jnp.maximum(-moved, 0.0)


def all_moved(x, step, g):
    moved = x - step * g
    contact = moved[:, LOW:HIGH]
    x = jnp.concatenate([moved[:, :LOW], jnp.maximum(contact, 0.0), moved[:, HIGH:]], axis=1)
    return x, jnp.maximum(-contact, 0.0)


def advance(sums, own, others, mate, near, far, statics, rows, coarse):
    _, step = step_of(sums)
    x, g, image = own
    x, lift = all_moved(x, step, g)
    mate_x, mate_g, near_x, far_x, near_face, far_face = others
    mate_kernel, near_kernel, far_kernel = coarse
    mate_x, mate_lift = moved_by(mate_x, step, mate_g)
    near_x, near_lift = moved_by(near_x, step, near[:, BLK:])
    far_x, far_lift = moved_by(far_x, step, far[:, BLK:])
    part, mate_part = contact_terms(lift, mate_lift, statics, True)
    mate_g = mate_g - step * mate + fine_dot(mate_lift, mate_kernel[...]) + mate_part
    near_face = near_face - step * near[:, :BLK] + fine_dot(near_lift, near_kernel[...])
    far_face = far_face - step * far[:, :BLK] + fine_dot(far_lift, far_kernel[...])
    lifted = whole_dot(lift, [(start - LOW, size, piece) for start, size, piece in rows()])
    g = g - step * image + lifted
    g = jnp.concatenate([g[:, :LOW], g[:, LOW:HIGH] + part, g[:, HIGH:]], axis=1)
    return x, g, [mate_x, mate_g, near_x, far_x, near_face, far_face]


CHUNK = 256
STARTS = (LOW, LOW + CHUNK) + (0,) + tuple(range(HIGH, M, CHUNK))


def whole_copy(dual_hbm, dual_ref, sems):
    copies = []
    for index, start in enumerate(STARTS):
        rows = pl.ds(start, CHUNK)
        copies.append(
            pltpu.make_async_copy(dual_hbm.at[rows], dual_ref.at[rows], sems.at[index])
        )
    for copy in copies:
        copy.start()

    def piece(index, wait):
        def read():
            if wait:
                copies[index].wait()
            return dual_ref[pl.ds(STARTS[index], CHUNK), :]

        return (STARTS[index], CHUNK, read)

    return piece


TABLE = 4 * CASES
SLOTS = TABLE + CASES
QUARTER = SLOTS + BLK
PACKED = QUARTER + BLK
SIDE = 12 * CASES


def is_even():
    return lax.rem(lax.axis_index("sub"), 2) == 0


def halves(block):
    high = block.astype(bf16)
    return high, (block - high.astype(f32)).astype(bf16)


def prepare_kernel(*refs):
    ids, count, x_ref, right_ref, mortar, dual_hbm = refs[:6]
    q_ref, packed, near_ref, far_ref, dual_ref, sems = refs[6:]
    piece = whole_copy(dual_hbm, dual_ref, sems)
    even = is_even()
    for k in range(4):
        packed[SLOTS:QUARTER, k * BLK : (k + 1) * BLK] = mortar[k * BLK : (k + 1) * BLK, :]
    table = slot_table(ids, count).astype(bf16)
    packed[TABLE:SLOTS, :] = jnp.concatenate([table] * 4, axis=1)
    x = x_ref[...]
    q = whole_dot(x, [piece(k, True) for k in range(len(STARTS))]) - right_ref[...]
    q_ref[...] = q
    start = pl.multiple_of(LOW + lax.rem(lax.axis_index("case"), 4) * BLK, BLK)
    packed[QUARTER:, :] = dual_ref[pl.ds(start, BLK), LOW:HIGH]
    parts = halves(x[:, LOW:HIGH]) + halves(q[:, LOW:HIGH])
    for k, part in enumerate(parts):
        packed[k * CASES : (k + 1) * CASES, :] = part
    contacts = split(x[:, LOW:HIGH])
    both = [(near_ref,), (far_ref,)]
    for (ref,), face, grad in zip(both, faces_of(x, even), faces_of(q, even)):
        for k, block in enumerate([face, grad] + contacts):
            high, low = halves(block)
            ref[2 * k * CASES : (2 * k + 1) * CASES, :] = high
            ref[(2 * k + 1) * CASES : (2 * k + 2) * CASES, :] = low
    first, second = dual_ref[LOW:HIGH, :BLK], dual_ref[LOW:HIGH, BLK:LOW]
    near_ref[SIDE:, :] = chosen(even, second, first)
    far_ref[SIDE:, :] = chosen(even, first, second)


def statics_of(ids, count, mortar, packed):
    own = [mortar[k * BLK : (k + 1) * BLK, :] for k in range(4)]
    mate = [packed[SLOTS:QUARTER, k * BLK : (k + 1) * BLK] for k in range(4)]
    mate_table = packed[TABLE:SLOTS, :BLK].astype(f32)
    return slots(slot_table(ids, count)), own, slots(mate_table), mate


def side_values(ref):
    parts = [ref[k * CASES : (k + 1) * CASES, :].astype(f32) for k in range(12)]
    return jnp.concatenate([parts[2 * k] + parts[2 * k + 1] for k in range(6)], axis=1)


def emit(outs, x, g, image, row, others):
    own_out, others_out, row_out, mate_out, near_out, far_out = outs
    row_out[...] = jnp.broadcast_to(row, row_out.shape)
    own_out[:, :M] = x
    own_out[:, M : 2 * M] = g
    own_out[:, 2 * M :] = image
    others_out[...] = jnp.concatenate(others, axis=1)
    mate_out[...] = image[:, LOW:HIGH]
    contact = g[:, LOW:HIGH]
    for ref, face in zip((near_out, far_out), faces_of(image, is_even())):
        ref[:, :BLK] = face
        ref[:, BLK:] = contact


def begin_kernel(*refs):
    ids, count, x_ref, q_ref, near, far, mortar, packed, match, dual_hbm = refs[:10]
    outs, (dual_ref, sems) = refs[10:16], refs[16:]
    piece = whole_copy(dual_hbm, dual_ref, sems)
    even = is_even()
    statics = statics_of(ids, count, mortar, packed)
    pick = picks(match[...], even)
    x = x_ref[...]
    parts = [packed[k * CASES : (k + 1) * CASES, :].astype(f32) for k in range(4)]
    mate = parts[0] + parts[1], parts[2] + parts[3]
    sides = side_values(near), side_values(far)
    g, others = begin(x, q_ref[...], mate, *sides, statics, pick, even)
    pieces = [piece(k, True) for k in range(len(STARTS))]
    image, row = tail(g, others, statics, pick, even, pieces)
    emit(outs, x, g, image, row, others)


WIDTHS = (CONTACT, CONTACT, CONTACT, CONTACT, BLK, BLK)


def advance_kernel(*refs):
    ids, count, sums, own, others, mate, near, far, mortar, packed, match = refs[:11]
    mate_kernel, near_kernel, far_kernel, dual_hbm = refs[11:15]
    outs, (dual_ref, sems) = refs[15:21], refs[21:]
    piece = whole_copy(dual_hbm, dual_ref, sems)
    even = is_even()
    statics = statics_of(ids, count, mortar, packed)
    pick = picks(match[...], even)

    def rows():
        return [piece(k, True) for k in range(2)]

    offsets = [sum(WIDTHS[:k]) for k in range(len(WIDTHS))]
    x, g, others = advance(
        sums[...],
        (own[:, :M], own[:, M : 2 * M], own[:, 2 * M :]),
        [others[:, start : start + size] for start, size in zip(offsets, WIDTHS)],
        mate[...],
        near[...],
        far[...],
        statics,
        rows,
        (mate_kernel, near_kernel.at[SIDE:], far_kernel.at[SIDE:]),
    )
    pieces = [piece(k, k >= 2) for k in range(len(STARTS))]
    image, row = tail(g, others, statics, pick, even, pieces)
    emit(outs, x, g, image, row, others)


def finish_kernel(sums, own, x_out, norm_out):
    norm, step = step_of(sums[...])
    x, _ = all_moved(own[:, :M], step, own[:, M : 2 * M])
    x_out[...] = x
    norm_out[...] = jnp.broadcast_to(jnp.sum(norm, axis=0, keepdims=True), norm_out.shape)


VMEM_SPEC = pl.BlockSpec(memory_space=pltpu.VMEM)
SMEM_SPEC = pl.BlockSpec(memory_space=pltpu.SMEM)
HBM_SPEC = pl.BlockSpec(memory_space=pltpu.HBM)


def call(kernel, specs, shapes, operands, scratch=True, grant=52):
    scratch_shapes = [pltpu.VMEM((M, M), bf16), pltpu.SemaphoreType.DMA((len(STARTS),))] if scratch else []
    return pl.pallas_call(
        kernel,
        in_specs=specs,
        out_specs=[VMEM_SPEC] * len(shapes),
        out_shape=[jax.ShapeDtypeStruct(shape, kind) for shape, kind in shapes],
        scratch_shapes=scratch_shapes,
        compiler_params=pltpu.CompilerParams(vmem_limit_bytes=grant << 20),
    )(*operands)


def swapped(value, other):
    devices = lax.axis_size("sub")
    return lax.ppermute(value, "sub", [(i, other(i) % devices) for i in range(devices)])


def with_mate(value):
    half_axis = lax.axis_size("sub") // 2
    return swapped(value, lambda i: i + half_axis)


def with_near(value):
    return swapped(value, lambda i: i ^ 1)


def with_far(value):
    return swapped(value, lambda i: i + 1 if i % 2 else i - 1)


def spread_sums(copies, axis):
    devices = lax.axis_size(axis)
    rows = lax.all_to_all(copies.reshape(devices, 1, BLK), axis, 0, 0)
    return rows.reshape(devices, BLK)


def on_device(multipliers, right_side, dual_ops, glue_match, mortar, contact_ids, contact_count):
    devices = lax.axis_size("sub")
    mortar = mortar.reshape(CONTACT, BLK)
    match = glue_match[0]
    scalars = [SMEM_SPEC, SMEM_SPEC]

    q, packed, to_near, to_far = call(
        prepare_kernel,
        scalars + [VMEM_SPEC] * 3 + [HBM_SPEC],
        [
            ((CASES, M), f32),
            ((PACKED, CONTACT), bf16),
            ((SIDE + CONTACT, BLK), bf16),
            ((SIDE + CONTACT, BLK), bf16),
        ],
        (contact_ids, contact_count, multipliers, right_side, mortar, dual_ops),
        grant=PREPARE_GRANT,
    )
    packed = with_mate(packed)
    near = near_kernel = with_near(to_near)
    far = far_kernel = with_far(to_far)
    cases = lax.axis_size("case")
    quarter = packed[QUARTER:]
    quarters = jnp.broadcast_to(quarter[None], (cases,) + quarter.shape)
    quarters = lax.all_to_all(quarters, "case", 0, 0)
    mate_kernel = quarters.reshape(cases * BLK, CONTACT)

    shapes = [
        ((CASES, 3 * M), f32),
        ((CASES, sum(WIDTHS)), f32),
        ((devices, BLK), f32),
        ((CASES, CONTACT), f32),
        ((CASES, BLK + CONTACT), f32),
        ((CASES, BLK + CONTACT), f32),
    ]
    own, others, copies, to_mate, to_near, to_far = call(
        begin_kernel,
        scalars + [VMEM_SPEC] * 7 + [HBM_SPEC],
        shapes,
        (
            contact_ids, contact_count, multipliers, q, near, far, mortar, packed, match,
            dual_ops,
        ),
    )
    copies, mate_kernel = lax.optimization_barrier((copies, mate_kernel))
    for _ in range(1, ITERS):
        sums = spread_sums(copies, "sub")
        mate = with_mate(to_mate)
        far = with_far(to_far)
        near = with_near(to_near)
        own, others, copies, to_mate, to_near, to_far = call(
            advance_kernel,
            scalars + [VMEM_SPEC] * 12 + [HBM_SPEC],
            shapes,
            (
                contact_ids, contact_count, sums, own, others, mate, near, far, mortar,
                packed, match, mate_kernel, near_kernel, far_kernel, dual_ops,
            ),
        )
    sums = spread_sums(copies, "sub")
    x, norm = call(
        finish_kernel,
        [VMEM_SPEC, VMEM_SPEC],
        [((CASES, M), f32), ((lax.axis_size("case"), BLK), f32)],
        (sums, own),
        scratch=False,
        grant=16,
    )
    total = spread_sums(norm, "case").sum(0)
    return (x, jnp.sqrt(total[:1]))


PREPARE_GRANT = 60


def solution(mesh):
    in_specs = (
        P("case", "sub"),
        P("case", "sub"),
        P("sub", None),
        P("sub", None, None),
        P("sub", None, None, None),
        P("sub", None),
        P("sub"),
    )
    out_specs = (P("case", "sub"), P())
    return jax.shard_map(
        on_device, mesh=mesh, in_specs=in_specs, out_specs=out_specs, check_vma=False
    )
```

```python
import jax
import jax.numpy as jnp
from jax import lax
from jax.experimental import pallas as pl
from jax.experimental.pallas import tpu as pltpu
from jax.sharding import PartitionSpec as P

M = 1536
BLK = 128
ITERS = 4
CASES = 16
LOW, HIGH = 2 * BLK, 6 * BLK
CONTACT = HIGH - LOW

penalty = 0.5
f32, bf16 = jnp.float32, jnp.bfloat16


def dot(value, matrix, transposed=False):
    contract = 1 if transposed else 0
    return lax.dot_general(
        value, matrix, (((1,), (contract,)), ((), ())), preferred_element_type=f32
    )


def fine_dot(value, matrix, transposed=False):
    high = value.astype(bf16)
    low = (value - high.astype(f32)).astype(bf16)
    both = dot(jnp.concatenate([high, low], axis=0), matrix, transposed)
    return both[:CASES] + both[CASES:]


def split(value):
    return [value[:, k * BLK : (k + 1) * BLK] for k in range(value.shape[1] // BLK)]


def weighed(weights, values):
    total = weights[0] * values[0]
    for weight, value in zip(weights[1:], values[1:]):
        total = total + weight * value
    return total


def slots(meta):
    onehot = [[meta[:, 4 * k + b : 4 * k + b + 1] for b in range(4)] for k in range(4)]
    active = [meta[:, 16 + k : 17 + k] for k in range(4)]
    return onehot, active


def slot_table(ids, count):
    lane = lax.broadcasted_iota(jnp.int32, (CASES, BLK), 1)
    table = jnp.zeros((CASES, BLK), f32)
    for k in range(4):
        table = jnp.where(lane == ids[0, k] + 4 * k, 1.0, table)
        alive = jnp.where(count[0] > k, 1.0, 0.0).astype(f32)
        table = jnp.where(lane == 16 + k, alive, table)
    return table


def jump_of(slave, own, terms, mortar):
    onehot, active = terms
    return [
        (fine_dot(weighed(onehot[k], slave), mortar[k]) - own[k]) * active[k] for k in range(4)
    ]


def reply_of(jump, terms, mortar):
    onehot, _ = terms
    rows = [fine_dot(jump[k], mortar[k], True) for k in range(4)]
    return [weighed([onehot[k][b] for k in range(4)], rows) for b in range(4)]


def contact_terms(own, mate, statics, both):
    terms, mortar, mate_terms, mate_mortar = statics[:4]
    own, mate = split(own), split(mate)
    jump = jump_of(mate, own, terms, mortar)
    mate_jump = jump_of(own, mate, mate_terms, mate_mortar)
    part = [r - j for r, j in zip(reply_of(mate_jump, mate_terms, mate_mortar), jump)]
    if not both:
        return jnp.concatenate(part, axis=1), None
    mate_part = [r - j for r, j in zip(reply_of(jump, terms, mortar), mate_jump)]
    return jnp.concatenate(part, axis=1), jnp.concatenate(mate_part, axis=1)


def chosen(even, first, second):
    return jnp.where(even, first, second)


def picks(match, even):
    rows = lax.broadcasted_iota(jnp.int32, (BLK, BLK), 0)
    first, second = match[0:1, :], match[1:2, :]
    sides = (chosen(even, second, first), chosen(even, first, second))
    return [jnp.where(rows == side, 1.0, 0.0).astype(bf16) for side in sides]


def faces_of(value, even):
    first, second = value[:, :BLK], value[:, BLK:LOW]
    return chosen(even, second, first), chosen(even, first, second)


def placed(near, far, even):
    return [chosen(even, far, near), chosen(even, near, far)]


def whole_dot(value, pieces):
    high = value.astype(bf16)
    low = (value - high.astype(f32)).astype(bf16)
    both, total = jnp.concatenate([high, low], axis=0), None
    for start, size, piece in pieces:
        part = dot(both[:, start : start + size], piece())
        total = part if total is None else total + part
    return total[:CASES] + total[CASES:]


def begin(x, q, mate, near, far, statics, pick, even):
    mate_x, mate_q = mate
    part, mate_part = contact_terms(x[:, LOW:HIGH], mate_x, statics, True)
    own = faces_of(x, even)
    glued, grads, contacts = [], [], []
    for side, face, matrix in zip((near, far), own, pick):
        side_x, side_q, contact = side[:, :BLK], side[:, BLK : 2 * BLK], side[:, 2 * BLK :]
        glued.append(penalty * (face - fine_dot(side_x, matrix)))
        grads.append(side_q + penalty * (side_x - fine_dot(face, matrix, True)))
        contacts.append(contact)
    faces = jnp.concatenate(placed(*glued, even), axis=1)
    g = jnp.concatenate(
        [q[:, :LOW] + faces, q[:, LOW:HIGH] + part, q[:, HIGH:]],
        axis=1,
    )
    return g, [mate_x, mate_q + mate_part] + contacts + grads


def tail(g, others, statics, pick, even, pieces):
    part, _ = contact_terms(g[:, LOW:HIGH], others[1], statics, False)
    glued = [
        penalty * (face - fine_dot(side, matrix))
        for face, side, matrix in zip(faces_of(g, even), others[4:], pick)
    ]
    zeros = jnp.zeros((CASES, M - HIGH), f32)
    image = whole_dot(g, pieces)
    image = image + jnp.concatenate(placed(*glued, even) + [part, zeros], axis=1)
    norm = jnp.sum(g * g, axis=1, keepdims=True)
    curve = jnp.sum(g * image, axis=1, keepdims=True)
    lane = lax.broadcasted_iota(jnp.int32, (CASES, BLK), 1)
    row = lax.broadcasted_iota(jnp.int32, (CASES, BLK), 0)
    spread = jnp.where(lane == row, norm, 0.0) + jnp.where(lane == row + CASES, curve, 0.0)
    return image, jnp.sum(spread, axis=0, keepdims=True)


def step_of(sums):
    total = jnp.sum(sums, axis=0, keepdims=True)
    lane = lax.broadcasted_iota(jnp.int32, (CASES, BLK), 1)
    row = lax.broadcasted_iota(jnp.int32, (CASES, BLK), 0)
    norm = jnp.sum(jnp.where(lane == row, total, 0.0), axis=1, keepdims=True)
    curve = jnp.sum(jnp.where(lane == row + CASES, total, 0.0), axis=1, keepdims=True)
    return norm, norm / curve


def moved_by(x, step, g):
    moved = x - step * g
    return jnp.maximum(moved, 0.0), jnp.maximum(-moved, 0.0)


def all_moved(x, step, g):
    moved = x - step * g
    contact = moved[:, LOW:HIGH]
    x = jnp.concatenate([moved[:, :LOW], jnp.maximum(contact, 0.0), moved[:, HIGH:]], axis=1)
    return x, jnp.maximum(-contact, 0.0)


def advance(sums, own, others, mate, near, far, statics, rows, coarse):
    _, step = step_of(sums)
    x, g, image = own
    x, lift = all_moved(x, step, g)
    mate_x, mate_g, near_x, far_x, near_face, far_face = others
    mate_kernel, near_kernel, far_kernel = coarse
    mate_x, mate_lift = moved_by(mate_x, step, mate_g)
    near_x, near_lift = moved_by(near_x, step, near[:, BLK:])
    far_x, far_lift = moved_by(far_x, step, far[:, BLK:])
    part, mate_part = contact_terms(lift, mate_lift, statics, True)
    mate_g = mate_g - step * mate + symmetric_dot(mate_lift, mate_kernel) + mate_part
    near_face = near_face - step * near[:, :BLK] + fine_dot(near_lift, near_kernel[...])
    far_face = far_face - step * far[:, :BLK] + fine_dot(far_lift, far_kernel[...])
    lifted = whole_dot(lift, rows)
    g = g - step * image + lifted
    g = jnp.concatenate([g[:, :LOW], g[:, LOW:HIGH] + part, g[:, HIGH:]], axis=1)
    return x, g, [mate_x, mate_g, near_x, far_x, near_face, far_face]


CHUNK = 256
STARTS = (LOW, LOW + CHUNK) + (0,) + tuple(range(HIGH, M, CHUNK))


def whole_copy(dual_hbm, dual_ref, sems, starts=None):
    copies = []
    for index, start in enumerate(starts or STARTS):
        span = pl.ds(start, CHUNK)
        copies.append(
            pltpu.make_async_copy(dual_hbm.at[span], dual_ref.at[span], sems.at[index])
        )
    for copy in copies:
        copy.start()

    def piece(index, wait):
        def read():
            if wait:
                copies[index].wait()
            return dual_ref[pl.ds(STARTS[index], CHUNK), :]

        return (STARTS[index], CHUNK, read)

    return piece


TABLE = 4 * CASES
SLOTS = TABLE + CASES
UPPER = SLOTS + BLK
PACKED = UPPER + 2 * BLK + BLK // 2
SIDE = 12 * CASES


def is_even():
    return lax.rem(lax.axis_index("sub"), 2) == 0


def halves(block):
    high = block.astype(bf16)
    return high, (block - high.astype(f32)).astype(bf16)


def upper_places():
    half = BLK // 2
    places = {}
    for k in range(4):
        places[0, k] = [(UPPER, BLK, k)]
    for k in range(1, 4):
        places[1, k] = [(UPPER + BLK, BLK, k)]
    places[3, 3] = [(UPPER + BLK, BLK, 0)]
    for k in (2, 3):
        lane = 2 * (k - 2)
        places[2, k] = [(UPPER + 2 * BLK, half, lane), (UPPER + 2 * BLK, half, lane + 1)]
    return places


def store_upper(packed, dual_ref):
    for (i, j), places in upper_places().items():
        start = LOW + i * BLK
        for row, size, lane in places:
            block = dual_ref[start : start + size, LOW + j * BLK : LOW + (j + 1) * BLK]
            packed[row : row + size, lane * BLK : (lane + 1) * BLK] = block
            start = start + size


def symmetric_dot(value, packed):
    high, low = halves(value)
    both = split(jnp.concatenate([high, low], axis=0))
    blocks = {}
    for key, places in upper_places().items():
        parts = [packed[row : row + n, lane * BLK : (lane + 1) * BLK] for row, n, lane in places]
        blocks[key] = parts[0] if len(parts) == 1 else jnp.concatenate(parts, axis=0)
    outs = []
    for j in range(4):
        total = None
        for i in range(4):
            part = dot(both[i], blocks[min(i, j), max(i, j)], i > j)
            total = part if total is None else total + part
        outs.append(total[:CASES] + total[CASES:])
    return jnp.concatenate(outs, axis=1)


def prepare_kernel(*refs):
    ids, count, x_ref, right_ref, mortar, dual_hbm = refs[:6]
    q_ref, packed, near_ref, far_ref, dual_ref, sems = refs[6:]
    piece = whole_copy(dual_hbm, dual_ref, sems)
    even = is_even()
    for k in range(4):
        packed[SLOTS:UPPER, k * BLK : (k + 1) * BLK] = mortar[k * BLK : (k + 1) * BLK, :]
    table = slot_table(ids, count).astype(bf16)
    packed[TABLE:SLOTS, :] = jnp.concatenate([table] * 4, axis=1)
    x = x_ref[...]
    q = whole_dot(x, [piece(k, True) for k in range(len(STARTS))]) - right_ref[...]
    q_ref[...] = q
    store_upper(packed, dual_ref)
    parts = halves(x[:, LOW:HIGH]) + halves(q[:, LOW:HIGH])
    for k, part in enumerate(parts):
        packed[k * CASES : (k + 1) * CASES, :] = part
    contacts = split(x[:, LOW:HIGH])
    both = [(near_ref,), (far_ref,)]
    for (ref,), face, grad in zip(both, faces_of(x, even), faces_of(q, even)):
        for k, block in enumerate([face, grad] + contacts):
            high, low = halves(block)
            ref[2 * k * CASES : (2 * k + 1) * CASES, :] = high
            ref[(2 * k + 1) * CASES : (2 * k + 2) * CASES, :] = low
    first, second = dual_ref[LOW:HIGH, :BLK], dual_ref[LOW:HIGH, BLK:LOW]
    near_ref[SIDE:, :] = chosen(even, second, first)
    far_ref[SIDE:, :] = chosen(even, first, second)


def statics_of(ids, count, mortar, packed):
    own = [mortar[k * BLK : (k + 1) * BLK, :] for k in range(4)]
    mate = [packed[SLOTS:UPPER, k * BLK : (k + 1) * BLK] for k in range(4)]
    mate_table = packed[TABLE:SLOTS, :BLK].astype(f32)
    return slots(slot_table(ids, count)), own, slots(mate_table), mate


def side_values(ref):
    parts = [ref[k * CASES : (k + 1) * CASES, :].astype(f32) for k in range(12)]
    return jnp.concatenate([parts[2 * k] + parts[2 * k + 1] for k in range(6)], axis=1)


def emit(outs, x, g, image, row, others):
    own_out, others_out, row_out, mate_out, near_out, far_out = outs
    row_out[...] = jnp.broadcast_to(row, row_out.shape)
    own_out[:, :M] = x
    own_out[:, M : 2 * M] = g
    own_out[:, 2 * M :] = image
    others_out[...] = jnp.concatenate(others, axis=1)
    mate_out[...] = image[:, LOW:HIGH]
    contact = g[:, LOW:HIGH]
    for ref, face in zip((near_out, far_out), faces_of(image, is_even())):
        ref[:, :BLK] = face
        ref[:, BLK:] = contact


def begin_kernel(*refs):
    ids, count, x_ref, q_ref, near, far, mortar, packed, match, dual_hbm = refs[:10]
    outs, (dual_ref, sems) = refs[10:16], refs[16:]
    piece = whole_copy(dual_hbm, dual_ref, sems)
    even = is_even()
    statics = statics_of(ids, count, mortar, packed)
    pick = picks(match[...], even)
    x = x_ref[...]
    parts = [packed[k * CASES : (k + 1) * CASES, :].astype(f32) for k in range(4)]
    mate = parts[0] + parts[1], parts[2] + parts[3]
    sides = side_values(near), side_values(far)
    g, others = begin(x, q_ref[...], mate, *sides, statics, pick, even)
    pieces = [piece(k, True) for k in range(len(STARTS))]
    image, row = tail(g, others, statics, pick, even, pieces)
    emit(outs, x, g, image, row, others)


WIDTHS = (CONTACT, CONTACT, CONTACT, CONTACT, BLK, BLK)


def advanced(refs, piece):
    ids, count, sums, own, others, mate, near, far, mortar, packed, _ = refs[:11]
    near_kernel, far_kernel = refs[11:13]
    statics = statics_of(ids, count, mortar, packed)
    offsets = [sum(WIDTHS[:k]) for k in range(len(WIDTHS))]
    lift_rows = [(k * CHUNK, CHUNK, piece(k, True)[2]) for k in range(2)]
    x, g, others = advance(
        sums[...],
        (own[:, :M], own[:, M : 2 * M], own[:, 2 * M :]),
        [others[:, start : start + size] for start, size in zip(offsets, WIDTHS)],
        mate[...],
        near[...],
        far[...],
        statics,
        lift_rows,
        (packed, near_kernel.at[SIDE:], far_kernel.at[SIDE:]),
    )
    return x, g, others, statics


def advance_kernel(*refs):
    dual_hbm, outs, (dual_ref, sems) = refs[13], refs[14:20], refs[20:]
    piece = whole_copy(dual_hbm, dual_ref, sems)
    even = is_even()
    x, g, others, statics = advanced(refs[:13], piece)
    pick = picks(refs[10][...], even)
    pieces = [piece(k, k >= 2) for k in range(len(STARTS))]
    image, row = tail(g, others, statics, pick, even, pieces)
    emit(outs, x, g, image, row, others)


def last_advance_kernel(*refs):
    dual_hbm, (own_out, others_out, row_out), (dual_ref, sems) = refs[13], refs[14:17], refs[17:]
    piece = whole_copy(dual_hbm, dual_ref, sems, STARTS[:2])
    x, g, others, _ = advanced(refs[:13], piece)
    own_out[:, :M] = x
    own_out[:, M:] = g
    others_out[...] = jnp.concatenate([others[1], others[4], others[5]], axis=1)
    total = jnp.sum(jnp.sum(g * g, axis=1, keepdims=True), axis=0, keepdims=True)
    row_out[...] = jnp.broadcast_to(total, row_out.shape)


def last_tail_kernel(*refs):
    ids, count, own, others, mortar, packed, match, dual_hbm = refs[:8]
    row_out, dual_ref, sems = refs[8:]
    piece = whole_copy(dual_hbm, dual_ref, sems)
    even = is_even()
    statics = statics_of(ids, count, mortar, packed)
    pick = picks(match[...], even)
    others = [
        None,
        others[:, :CONTACT],
        None,
        None,
        others[:, CONTACT : CONTACT + BLK],
        others[:, CONTACT + BLK :],
    ]
    pieces = [piece(k, True) for k in range(len(STARTS))]
    _, row = tail(own[:, M:], others, statics, pick, even, pieces)
    row_out[...] = jnp.broadcast_to(row, row_out.shape)


def finish_kernel(sums, own, x_out, norm_out):
    rows = sums[...]
    _, step = step_of(rows)
    x, _ = all_moved(own[:, :M], step, own[:, M : 2 * M])
    x_out[...] = x
    total = jnp.sum(rows, axis=0, keepdims=True)[:, 2 * CASES : 2 * CASES + 1]
    norm_out[...] = jnp.broadcast_to(jnp.sqrt(total), norm_out.shape)


VMEM_SPEC = pl.BlockSpec(memory_space=pltpu.VMEM)
SMEM_SPEC = pl.BlockSpec(memory_space=pltpu.SMEM)
HBM_SPEC = pl.BlockSpec(memory_space=pltpu.HBM)


def call(kernel, specs, shapes, operands, scratch=True, grant=52):
    scratch_shapes = [pltpu.VMEM((M, M), bf16), pltpu.SemaphoreType.DMA((len(STARTS),))] if scratch else []
    return pl.pallas_call(
        kernel,
        in_specs=specs,
        out_specs=[VMEM_SPEC] * len(shapes),
        out_shape=[jax.ShapeDtypeStruct(shape, kind) for shape, kind in shapes],
        scratch_shapes=scratch_shapes,
        compiler_params=pltpu.CompilerParams(vmem_limit_bytes=grant << 20),
    )(*operands)


def swapped(value, other):
    devices = lax.axis_size("sub")
    return lax.ppermute(value, "sub", [(i, other(i) % devices) for i in range(devices)])


def with_mate(value):
    half_axis = lax.axis_size("sub") // 2
    return swapped(value, lambda i: i + half_axis)


def with_near(value):
    return swapped(value, lambda i: i ^ 1)


def with_far(value):
    return swapped(value, lambda i: i + 1 if i % 2 else i - 1)


def spread_sums(copies, axis):
    devices = lax.axis_size(axis)
    rows = lax.all_to_all(copies.reshape(devices, 1, BLK), axis, 0, 0)
    return rows.reshape(devices, BLK)


def on_device(multipliers, right_side, dual_ops, glue_match, mortar, contact_ids, contact_count):
    devices = lax.axis_size("sub")
    mortar = mortar.reshape(CONTACT, BLK)
    match = glue_match[0]
    scalars = [SMEM_SPEC, SMEM_SPEC]

    q, packed, to_near, to_far = call(
        prepare_kernel,
        scalars + [VMEM_SPEC] * 3 + [HBM_SPEC],
        [
            ((CASES, M), f32),
            ((PACKED, CONTACT), bf16),
            ((SIDE + CONTACT, BLK), bf16),
            ((SIDE + CONTACT, BLK), bf16),
        ],
        (contact_ids, contact_count, multipliers, right_side, mortar, dual_ops),
        grant=PREPARE_GRANT,
    )
    packed = with_mate(packed)
    near = near_kernel = with_near(to_near)
    far = far_kernel = with_far(to_far)

    shapes = [
        ((CASES, 3 * M), f32),
        ((CASES, sum(WIDTHS)), f32),
        ((devices, BLK), f32),
        ((CASES, CONTACT), f32),
        ((CASES, BLK + CONTACT), f32),
        ((CASES, BLK + CONTACT), f32),
    ]
    own, others, copies, to_mate, to_near, to_far = call(
        begin_kernel,
        scalars + [VMEM_SPEC] * 7 + [HBM_SPEC],
        shapes,
        (
            contact_ids, contact_count, multipliers, q, near, far, mortar, packed, match,
            dual_ops,
        ),
    )
    for iteration in range(1, ITERS):
        sums = spread_sums(copies, "sub")
        mate = with_mate(to_mate)
        far = with_far(to_far)
        near = with_near(to_near)
        operands = (
            contact_ids, contact_count, sums, own, others, mate, near, far, mortar, packed,
            match, near_kernel, far_kernel, dual_ops,
        )
        if iteration < ITERS - 1:
            own, others, copies, to_mate, to_near, to_far = call(
                advance_kernel,
                scalars + [VMEM_SPEC] * 11 + [HBM_SPEC],
                shapes,
                operands,
            )
    cases = lax.axis_size("case")
    own, others, norms = call(
        last_advance_kernel,
        scalars + [VMEM_SPEC] * 11 + [HBM_SPEC],
        [
            ((CASES, 2 * M), f32),
            ((CASES, CONTACT + 2 * BLK), f32),
            ((cases, BLK), f32),
        ],
        operands,
    )
    norms = spread_sums(norms, "case")
    (copies,) = call(
        last_tail_kernel,
        scalars + [VMEM_SPEC] * 5 + [HBM_SPEC],
        [((devices, BLK), f32)],
        (contact_ids, contact_count, own, others, mortar, packed, match, dual_ops),
    )
    lane = lax.broadcasted_iota(jnp.int32, (1, BLK), 1)
    norm_row = jnp.where(lane == 2 * CASES, jnp.sum(norms, axis=0, keepdims=True), 0.0)
    sums = spread_sums(copies + norm_row, "sub")
    x, norm = call(
        finish_kernel,
        [VMEM_SPEC, VMEM_SPEC],
        [((CASES, M), f32), ((1, BLK), f32)],
        (sums, own),
        scratch=False,
        grant=16,
    )
    return (x, norm[0, :1])


PREPARE_GRANT = 60


def solution(mesh):
    in_specs = (
        P("case", "sub"),
        P("case", "sub"),
        P("sub", None),
        P("sub", None, None),
        P("sub", None, None, None),
        P("sub", None),
        P("sub"),
    )
    out_specs = (P("case", "sub"), P())
    return jax.shard_map(
        on_device, mesh=mesh, in_specs=in_specs, out_specs=out_specs, check_vma=False
    )
```

```python
import jax
import jax.numpy as jnp
from jax import lax
from jax.experimental import pallas as pl
from jax.experimental.pallas import tpu as pltpu
from jax.sharding import PartitionSpec as P

M = 1536
BLK = 128
ITERS = 4
CASES = 16
LOW, HIGH = 2 * BLK, 6 * BLK
CONTACT = HIGH - LOW

penalty = 0.5
f32, bf16 = jnp.float32, jnp.bfloat16


def dot(value, matrix, transposed=False):
    contract = 1 if transposed else 0
    return lax.dot_general(
        value, matrix, (((1,), (contract,)), ((), ())), preferred_element_type=f32
    )


def fine_dot(value, matrix, transposed=False):
    high = value.astype(bf16)
    low = (value - high.astype(f32)).astype(bf16)
    both = dot(jnp.concatenate([high, low], axis=0), matrix, transposed)
    return both[:CASES] + both[CASES:]


def split(value):
    return [value[:, k * BLK : (k + 1) * BLK] for k in range(value.shape[1] // BLK)]


def weighed(weights, values):
    total = weights[0] * values[0]
    for weight, value in zip(weights[1:], values[1:]):
        total = total + weight * value
    return total


def slots(meta):
    onehot = [[meta[:, 4 * k + b : 4 * k + b + 1] for b in range(4)] for k in range(4)]
    active = [meta[:, 16 + k : 17 + k] for k in range(4)]
    return onehot, active


def slot_table(ids, count):
    lane = lax.broadcasted_iota(jnp.int32, (CASES, BLK), 1)
    table = jnp.zeros((CASES, BLK), f32)
    for k in range(4):
        table = jnp.where(lane == ids[0, k] + 4 * k, 1.0, table)
        alive = jnp.where(count[0] > k, 1.0, 0.0).astype(f32)
        table = jnp.where(lane == 16 + k, alive, table)
    return table


def jump_of(slave, own, terms, mortar):
    onehot, active = terms
    return [
        (fine_dot(weighed(onehot[k], slave), mortar[k]) - own[k]) * active[k] for k in range(4)
    ]


def reply_of(jump, terms, mortar):
    onehot, _ = terms
    rows = [fine_dot(jump[k], mortar[k], True) for k in range(4)]
    return [weighed([onehot[k][b] for k in range(4)], rows) for b in range(4)]


def contact_terms(own, mate, statics, both):
    terms, mortar, mate_terms, mate_mortar = statics[:4]
    own, mate = split(own), split(mate)
    jump = jump_of(mate, own, terms, mortar)
    mate_jump = jump_of(own, mate, mate_terms, mate_mortar)
    part = [r - j for r, j in zip(reply_of(mate_jump, mate_terms, mate_mortar), jump)]
    if not both:
        return jnp.concatenate(part, axis=1), None
    mate_part = [r - j for r, j in zip(reply_of(jump, terms, mortar), mate_jump)]
    return jnp.concatenate(part, axis=1), jnp.concatenate(mate_part, axis=1)


def chosen(even, first, second):
    return jnp.where(even, first, second)


def picks(match, even):
    rows = lax.broadcasted_iota(jnp.int32, (BLK, BLK), 0)
    first, second = match[0:1, :], match[1:2, :]
    sides = (chosen(even, second, first), chosen(even, first, second))
    return [jnp.where(rows == side, 1.0, 0.0).astype(bf16) for side in sides]


def faces_of(value, even):
    first, second = value[:, :BLK], value[:, BLK:LOW]
    return chosen(even, second, first), chosen(even, first, second)


def placed(near, far, even):
    return [chosen(even, far, near), chosen(even, near, far)]


def whole_dot(value, pieces):
    high = value.astype(bf16)
    low = (value - high.astype(f32)).astype(bf16)
    both, total = jnp.concatenate([high, low], axis=0), None
    for start, size, piece in pieces:
        part = dot(both[:, start : start + size], piece())
        total = part if total is None else total + part
    return total[:CASES] + total[CASES:]


def begin(x, q, mate, near, far, statics, pick, even):
    mate_x, mate_q = mate
    part, mate_part = contact_terms(x[:, LOW:HIGH], mate_x, statics, True)
    own = faces_of(x, even)
    glued, grads, contacts = [], [], []
    for side, face, matrix in zip((near, far), own, pick):
        side_x, side_q, contact = side[:, :BLK], side[:, BLK : 2 * BLK], side[:, 2 * BLK :]
        glued.append(penalty * (face - fine_dot(side_x, matrix)))
        grads.append(side_q + penalty * (side_x - fine_dot(face, matrix, True)))
        contacts.append(contact)
    faces = jnp.concatenate(placed(*glued, even), axis=1)
    g = jnp.concatenate(
        [q[:, :LOW] + faces, q[:, LOW:HIGH] + part, q[:, HIGH:]],
        axis=1,
    )
    return g, [mate_x, mate_q + mate_part] + contacts + grads


def tail(g, others, statics, pick, even, pieces):
    part, _ = contact_terms(g[:, LOW:HIGH], others[1], statics, False)
    glued = [
        penalty * (face - fine_dot(side, matrix))
        for face, side, matrix in zip(faces_of(g, even), others[4:], pick)
    ]
    zeros = jnp.zeros((CASES, M - HIGH), f32)
    image = whole_dot(g, pieces)
    image = image + jnp.concatenate(placed(*glued, even) + [part, zeros], axis=1)
    norm = jnp.sum(g * g, axis=1, keepdims=True)
    curve = jnp.sum(g * image, axis=1, keepdims=True)
    lane = lax.broadcasted_iota(jnp.int32, (CASES, BLK), 1)
    row = lax.broadcasted_iota(jnp.int32, (CASES, BLK), 0)
    spread = jnp.where(lane == row, norm, 0.0) + jnp.where(lane == row + CASES, curve, 0.0)
    return image, jnp.sum(spread, axis=0, keepdims=True)


def step_of(sums):
    total = jnp.sum(sums, axis=0, keepdims=True)
    lane = lax.broadcasted_iota(jnp.int32, (CASES, BLK), 1)
    row = lax.broadcasted_iota(jnp.int32, (CASES, BLK), 0)
    norm = jnp.sum(jnp.where(lane == row, total, 0.0), axis=1, keepdims=True)
    curve = jnp.sum(jnp.where(lane == row + CASES, total, 0.0), axis=1, keepdims=True)
    return norm, norm / curve


def moved_by(x, step, g):
    moved = x - step * g
    return jnp.maximum(moved, 0.0), jnp.maximum(-moved, 0.0)


def all_moved(x, step, g):
    moved = x - step * g
    contact = moved[:, LOW:HIGH]
    x = jnp.concatenate([moved[:, :LOW], jnp.maximum(contact, 0.0), moved[:, HIGH:]], axis=1)
    return x, jnp.maximum(-contact, 0.0)


def advance(sums, own, others, mate, near, far, statics, rows, coarse):
    _, step = step_of(sums)
    x, g, image = own
    x, lift = all_moved(x, step, g)
    mate_x, mate_g, near_x, far_x, near_face, far_face = others
    mate_kernel, near_kernel, far_kernel = coarse
    mate_x, mate_lift = moved_by(mate_x, step, mate_g)
    near_x, near_lift = moved_by(near_x, step, near[:, BLK:])
    far_x, far_lift = moved_by(far_x, step, far[:, BLK:])
    part, mate_part = contact_terms(lift, mate_lift, statics, True)
    mate_g = mate_g - step * mate + quarters_dot(mate_lift, *mate_kernel) + mate_part
    near_face = near_face - step * near[:, :BLK] + fine_dot(near_lift, near_kernel[...])
    far_face = far_face - step * far[:, :BLK] + fine_dot(far_lift, far_kernel[...])
    lifted = whole_dot(lift, rows)
    g = g - step * image + lifted
    g = jnp.concatenate([g[:, :LOW], g[:, LOW:HIGH] + part, g[:, HIGH:]], axis=1)
    return x, g, [mate_x, mate_g, near_x, far_x, near_face, far_face]


CHUNK = 256
STARTS = (LOW, LOW + CHUNK) + (0,) + tuple(range(HIGH, M, CHUNK))


def whole_copy(dual_hbm, dual_ref, sems, starts=None):
    copies = []
    for index, start in enumerate(starts or STARTS):
        span = pl.ds(start, CHUNK)
        copies.append(
            pltpu.make_async_copy(dual_hbm.at[span], dual_ref.at[span], sems.at[index])
        )
    for copy in copies:
        copy.start()

    def piece(index, wait):
        def read():
            if wait:
                copies[index].wait()
            return dual_ref[pl.ds(STARTS[index], CHUNK), :]

        return (STARTS[index], CHUNK, read)

    return piece


TABLE = 2 * CASES
SLOTS = TABLE + CASES
PACKED = SLOTS + BLK
SIDE = 6 * CASES


def is_even():
    return lax.rem(lax.axis_index("sub"), 2) == 0


def halves(block):
    high = block.astype(bf16)
    return high, (block - high.astype(f32)).astype(bf16)


def quarters_dot(value, case, quarters):
    blocks, total = split(value), None
    for k in range(4):
        index = lax.bitwise_xor(case, k)
        block = blocks[0]
        for i in range(1, 4):
            block = jnp.where(index == i, blocks[i], block)
        part = dot(jnp.concatenate(halves(block), axis=0), quarters[k])
        total = part if total is None else total + part
    return total[:CASES] + total[CASES:]


def prepare_kernel(*refs):
    ids, count, x_ref, right_ref, mortar, dual_hbm = refs[:6]
    q_ref, packed, near_ref, far_ref, dual_ref, sems = refs[6:]
    piece = whole_copy(dual_hbm, dual_ref, sems)
    even = is_even()
    for k in range(4):
        packed[SLOTS:, k * BLK : (k + 1) * BLK] = mortar[k * BLK : (k + 1) * BLK, :]
    table = slot_table(ids, count).astype(bf16)
    packed[TABLE:SLOTS, :] = jnp.concatenate([table] * 4, axis=1)
    x = x_ref[...]
    q = whole_dot(x, [piece(k, True) for k in range(len(STARTS))]) - right_ref[...]
    q_ref[...] = q
    packed[:CASES, :] = x[:, LOW:HIGH].astype(bf16)
    packed[CASES:TABLE, :] = q[:, LOW:HIGH].astype(bf16)
    contacts = split(x[:, LOW:HIGH])
    both = [(near_ref,), (far_ref,)]
    for (ref,), face, grad in zip(both, faces_of(x, even), faces_of(q, even)):
        for k, block in enumerate([face, grad] + contacts):
            ref[k * CASES : (k + 1) * CASES, :] = block.astype(bf16)
    first, second = dual_ref[LOW:HIGH, :BLK], dual_ref[LOW:HIGH, BLK:LOW]
    near_ref[SIDE:, :] = chosen(even, second, first)
    far_ref[SIDE:, :] = chosen(even, first, second)


def statics_of(ids, count, mortar, packed):
    own = [mortar[k * BLK : (k + 1) * BLK, :] for k in range(4)]
    mate = [packed[SLOTS:, k * BLK : (k + 1) * BLK] for k in range(4)]
    mate_table = packed[TABLE:SLOTS, :BLK].astype(f32)
    return slots(slot_table(ids, count)), own, slots(mate_table), mate


def side_values(ref):
    parts = [ref[k * CASES : (k + 1) * CASES, :].astype(f32) for k in range(6)]
    return jnp.concatenate(parts, axis=1)


def emit(outs, x, g, image, row, others):
    own_out, others_out, row_out, mate_out, near_out, far_out = outs
    row_out[...] = jnp.broadcast_to(row, row_out.shape)
    own_out[:, :M] = x
    own_out[:, M : 2 * M] = g
    own_out[:, 2 * M :] = image
    others_out[...] = jnp.concatenate(others, axis=1)
    mate_out[...] = image[:, LOW:HIGH]
    contact = g[:, LOW:HIGH]
    for ref, face in zip((near_out, far_out), faces_of(image, is_even())):
        ref[:, :BLK] = face
        ref[:, BLK:] = contact


def begin_kernel(*refs):
    ids, count, x_ref, q_ref, near, far, mortar, packed, match, dual_hbm = refs[:10]
    outs, (dual_ref, sems) = refs[10:16], refs[16:]
    piece = whole_copy(dual_hbm, dual_ref, sems)
    even = is_even()
    statics = statics_of(ids, count, mortar, packed)
    pick = picks(match[...], even)
    x = x_ref[...]
    mate = packed[:CASES, :].astype(f32), packed[CASES:TABLE, :].astype(f32)
    sides = side_values(near), side_values(far)
    g, others = begin(x, q_ref[...], mate, *sides, statics, pick, even)
    pieces = [piece(k, True) for k in range(len(STARTS))]
    image, row = tail(g, others, statics, pick, even, pieces)
    emit(outs, x, g, image, row, others)


WIDTHS = (CONTACT, CONTACT, CONTACT, CONTACT, BLK, BLK)


def advanced(refs, piece):
    ids, count, sums, own, others, mate, near, far, mortar, packed, _ = refs[:11]
    near_kernel, far_kernel, quarter, second, pair = refs[11:16]
    quarters = (quarter[...], second[...], pair[:BLK, :], pair[BLK:, :])
    statics = statics_of(ids, count, mortar, packed)
    offsets = [sum(WIDTHS[:k]) for k in range(len(WIDTHS))]
    lift_rows = [(k * CHUNK, CHUNK, piece(k, True)[2]) for k in range(2)]
    x, g, others = advance(
        sums[...],
        (own[:, :M], own[:, M : 2 * M], own[:, 2 * M :]),
        [others[:, start : start + size] for start, size in zip(offsets, WIDTHS)],
        mate[...],
        near[...],
        far[...],
        statics,
        lift_rows,
        ((lax.axis_index("case"), quarters), near_kernel.at[SIDE:], far_kernel.at[SIDE:]),
    )
    return x, g, others, statics


def advance_kernel(*refs):
    dual_hbm, outs, (dual_ref, sems) = refs[16], refs[17:23], refs[23:]
    piece = whole_copy(dual_hbm, dual_ref, sems)
    even = is_even()
    x, g, others, statics = advanced(refs[:16], piece)
    pick = picks(refs[10][...], even)
    pieces = [piece(k, k >= 2) for k in range(len(STARTS))]
    image, row = tail(g, others, statics, pick, even, pieces)
    emit(outs, x, g, image, row, others)


def last_advance_kernel(*refs):
    dual_hbm, (own_out, others_out, row_out), (dual_ref, sems) = refs[16], refs[17:20], refs[20:]
    piece = whole_copy(dual_hbm, dual_ref, sems, STARTS[:2])
    x, g, others, _ = advanced(refs[:16], piece)
    own_out[:, :M] = x
    own_out[:, M:] = g
    others_out[...] = jnp.concatenate([others[1], others[4], others[5]], axis=1)
    total = jnp.sum(jnp.sum(g * g, axis=1, keepdims=True), axis=0, keepdims=True)
    row_out[...] = jnp.broadcast_to(total, row_out.shape)


def last_tail_kernel(*refs):
    ids, count, own, others, mortar, packed, match, dual_hbm = refs[:8]
    row_out, dual_ref, sems = refs[8:]
    piece = whole_copy(dual_hbm, dual_ref, sems)
    even = is_even()
    statics = statics_of(ids, count, mortar, packed)
    pick = picks(match[...], even)
    others = [
        None,
        others[:, :CONTACT],
        None,
        None,
        others[:, CONTACT : CONTACT + BLK],
        others[:, CONTACT + BLK :],
    ]
    pieces = [piece(k, True) for k in range(len(STARTS))]
    _, row = tail(own[:, M:], others, statics, pick, even, pieces)
    row_out[...] = jnp.broadcast_to(row, row_out.shape)


def finish_kernel(sums, own, x_out, norm_out):
    rows = sums[...]
    _, step = step_of(rows)
    x, _ = all_moved(own[:, :M], step, own[:, M : 2 * M])
    x_out[...] = x
    total = jnp.sum(rows, axis=0, keepdims=True)[:, 2 * CASES : 2 * CASES + 1]
    norm_out[...] = jnp.broadcast_to(jnp.sqrt(total), norm_out.shape)


VMEM_SPEC = pl.BlockSpec(memory_space=pltpu.VMEM)
SMEM_SPEC = pl.BlockSpec(memory_space=pltpu.SMEM)
HBM_SPEC = pl.BlockSpec(memory_space=pltpu.HBM)


def call(kernel, specs, shapes, operands, scratch=True, grant=52):
    scratch_shapes = [pltpu.VMEM((M, M), bf16), pltpu.SemaphoreType.DMA((len(STARTS),))] if scratch else []
    return pl.pallas_call(
        kernel,
        in_specs=specs,
        out_specs=[VMEM_SPEC] * len(shapes),
        out_shape=[jax.ShapeDtypeStruct(shape, kind) for shape, kind in shapes],
        scratch_shapes=scratch_shapes,
        compiler_params=pltpu.CompilerParams(vmem_limit_bytes=grant << 20),
    )(*operands)


def swapped(value, other):
    devices = lax.axis_size("sub")
    return lax.ppermute(value, "sub", [(i, other(i) % devices) for i in range(devices)])


def with_mate(value):
    half_axis = lax.axis_size("sub") // 2
    return swapped(value, lambda i: i + half_axis)


def with_near(value):
    return swapped(value, lambda i: i ^ 1)


def with_far(value):
    return swapped(value, lambda i: i + 1 if i % 2 else i - 1)


def with_case(value, bit):
    cases = lax.axis_size("case")
    return lax.ppermute(value, "case", [(i, i ^ bit) for i in range(cases)])


def spread_sums(copies, axis):
    devices = lax.axis_size(axis)
    rows = lax.all_to_all(copies.reshape(devices, 1, BLK), axis, 0, 0)
    return rows.reshape(devices, BLK)


def on_device(multipliers, right_side, dual_ops, glue_match, mortar, contact_ids, contact_count):
    devices = lax.axis_size("sub")
    mortar = mortar.reshape(CONTACT, BLK)
    match = glue_match[0]
    scalars = [SMEM_SPEC, SMEM_SPEC]

    q, packed, to_near, to_far = call(
        prepare_kernel,
        scalars + [VMEM_SPEC] * 3 + [HBM_SPEC],
        [
            ((CASES, M), f32),
            ((PACKED, CONTACT), bf16),
            ((SIDE + CONTACT, BLK), bf16),
            ((SIDE + CONTACT, BLK), bf16),
        ],
        (contact_ids, contact_count, multipliers, right_side, mortar, dual_ops),
        grant=PREPARE_GRANT,
    )
    packed, dual_later = lax.optimization_barrier((packed, dual_ops))
    packed = with_mate(packed)
    near = near_kernel = with_near(to_near)
    far = far_kernel = with_far(to_far)
    start = LOW + lax.rem(lax.axis_index("case"), 4) * BLK
    quarter = lax.dynamic_slice(dual_later, (start, LOW), (BLK, CONTACT))
    quarter = with_mate(quarter)
    shapes = [
        ((CASES, 3 * M), f32),
        ((CASES, sum(WIDTHS)), f32),
        ((devices, BLK), f32),
        ((CASES, CONTACT), f32),
        ((CASES, BLK + CONTACT), f32),
        ((CASES, BLK + CONTACT), f32),
    ]
    own, others, copies, to_mate, to_near, to_far = call(
        begin_kernel,
        scalars + [VMEM_SPEC] * 7 + [HBM_SPEC],
        shapes,
        (
            contact_ids, contact_count, multipliers, q, near, far, mortar, packed, match,
            dual_ops,
        ),
    )
    for iteration in range(1, ITERS):
        sums = spread_sums(copies, "sub")
        mate = with_mate(to_mate)
        far = with_far(to_far)
        near = with_near(to_near)
        if iteration == 1:
            second = with_case(quarter, 1)
            pair = with_case(jnp.concatenate([quarter, second]), 2)
        operands = (
            contact_ids, contact_count, sums, own, others, mate, near, far, mortar, packed,
            match, near_kernel, far_kernel, quarter, second, pair, dual_ops,
        )
        if iteration < ITERS - 1:
            own, others, copies, to_mate, to_near, to_far = call(
                advance_kernel,
                scalars + [VMEM_SPEC] * 14 + [HBM_SPEC],
                shapes,
                operands,
            )
    cases = lax.axis_size("case")
    own, others, norms = call(
        last_advance_kernel,
        scalars + [VMEM_SPEC] * 14 + [HBM_SPEC],
        [
            ((CASES, 2 * M), f32),
            ((CASES, CONTACT + 2 * BLK), f32),
            ((cases, BLK), f32),
        ],
        operands,
    )
    norms = spread_sums(norms, "case")
    (copies,) = call(
        last_tail_kernel,
        scalars + [VMEM_SPEC] * 5 + [HBM_SPEC],
        [((devices, BLK), f32)],
        (contact_ids, contact_count, own, others, mortar, packed, match, dual_ops),
    )
    lane = lax.broadcasted_iota(jnp.int32, (1, BLK), 1)
    norm_row = jnp.where(lane == 2 * CASES, jnp.sum(norms, axis=0, keepdims=True), 0.0)
    sums = spread_sums(copies + norm_row, "sub")
    x, norm = call(
        finish_kernel,
        [VMEM_SPEC, VMEM_SPEC],
        [((CASES, M), f32), ((1, BLK), f32)],
        (sums, own),
        scratch=False,
        grant=16,
    )
    return (x, norm[0, :1])


PREPARE_GRANT = 60


def solution(mesh):
    in_specs = (
        P("case", "sub"),
        P("case", "sub"),
        P("sub", None),
        P("sub", None, None),
        P("sub", None, None, None),
        P("sub", None),
        P("sub"),
    )
    out_specs = (P("case", "sub"), P())
    return jax.shard_map(
        on_device, mesh=mesh, in_specs=in_specs, out_specs=out_specs, check_vma=False
    )
```

```python
import jax
import jax.numpy as jnp
from jax import lax
from jax.experimental import pallas as pl
from jax.experimental.pallas import tpu as pltpu
from jax.sharding import PartitionSpec as P

M = 1536
BLK = 128
ITERS = 4
CASES = 16
LOW, HIGH = 2 * BLK, 6 * BLK
CONTACT = HIGH - LOW

penalty = 0.5
f32, bf16 = jnp.float32, jnp.bfloat16


def dot(value, matrix, transposed=False):
    contract = 1 if transposed else 0
    return lax.dot_general(
        value, matrix, (((1,), (contract,)), ((), ())), preferred_element_type=f32
    )


def fine_dot(value, matrix, transposed=False):
    high = value.astype(bf16)
    low = (value - high.astype(f32)).astype(bf16)
    both = dot(jnp.concatenate([high, low], axis=0), matrix, transposed)
    return both[:CASES] + both[CASES:]


def split(value):
    return [value[:, k * BLK : (k + 1) * BLK] for k in range(value.shape[1] // BLK)]


def weighed(weights, values):
    total = weights[0] * values[0]
    for weight, value in zip(weights[1:], values[1:]):
        total = total + weight * value
    return total


def slots(meta):
    onehot = [[meta[:, 4 * k + b : 4 * k + b + 1] for b in range(4)] for k in range(4)]
    active = [meta[:, 16 + k : 17 + k] for k in range(4)]
    return onehot, active


def slot_table(ids, count):
    lane = lax.broadcasted_iota(jnp.int32, (CASES, BLK), 1)
    table = jnp.zeros((CASES, BLK), f32)
    for k in range(4):
        table = jnp.where(lane == ids[0, k] + 4 * k, 1.0, table)
        alive = jnp.where(count[0] > k, 1.0, 0.0).astype(f32)
        table = jnp.where(lane == 16 + k, alive, table)
    return table


def jump_of(slave, own, terms, mortar):
    onehot, active = terms
    return [
        (fine_dot(weighed(onehot[k], slave), mortar[k]) - own[k]) * active[k] for k in range(4)
    ]


def reply_of(jump, terms, mortar):
    onehot, _ = terms
    rows = [fine_dot(jump[k], mortar[k], True) for k in range(4)]
    return [weighed([onehot[k][b] for k in range(4)], rows) for b in range(4)]


def contact_terms(own, mate, statics, both):
    terms, mortar, mate_terms, mate_mortar = statics[:4]
    own, mate = split(own), split(mate)
    jump = jump_of(mate, own, terms, mortar)
    mate_jump = jump_of(own, mate, mate_terms, mate_mortar)
    part = [r - j for r, j in zip(reply_of(mate_jump, mate_terms, mate_mortar), jump)]
    if not both:
        return jnp.concatenate(part, axis=1), None
    mate_part = [r - j for r, j in zip(reply_of(jump, terms, mortar), mate_jump)]
    return jnp.concatenate(part, axis=1), jnp.concatenate(mate_part, axis=1)


def chosen(even, first, second):
    return jnp.where(even, first, second)


def picks(match, even):
    rows = lax.broadcasted_iota(jnp.int32, (BLK, BLK), 0)
    first, second = match[0:1, :], match[1:2, :]
    sides = (chosen(even, second, first), chosen(even, first, second))
    return [jnp.where(rows == side, 1.0, 0.0).astype(bf16) for side in sides]


def faces_of(value, even):
    first, second = value[:, :BLK], value[:, BLK:LOW]
    return chosen(even, second, first), chosen(even, first, second)


def placed(near, far, even):
    return [chosen(even, far, near), chosen(even, near, far)]


def whole_dot(value, pieces):
    high = value.astype(bf16)
    low = (value - high.astype(f32)).astype(bf16)
    both, total = jnp.concatenate([high, low], axis=0), None
    for start, size, piece in pieces:
        part = dot(both[:, start : start + size], piece())
        total = part if total is None else total + part
    return total[:CASES] + total[CASES:]


def begin(x, q, mate, near, far, statics, pick, even):
    mate_x, mate_q = mate
    part, mate_part = contact_terms(x[:, LOW:HIGH], mate_x, statics, True)
    own = faces_of(x, even)
    glued, grads, contacts = [], [], []
    for side, face, matrix in zip((near, far), own, pick):
        side_x, side_q, contact = side[:, :BLK], side[:, BLK : 2 * BLK], side[:, 2 * BLK :]
        glued.append(penalty * (face - fine_dot(side_x, matrix)))
        grads.append(side_q + penalty * (side_x - fine_dot(face, matrix, True)))
        contacts.append(contact)
    faces = jnp.concatenate(placed(*glued, even), axis=1)
    g = jnp.concatenate(
        [q[:, :LOW] + faces, q[:, LOW:HIGH] + part, q[:, HIGH:]],
        axis=1,
    )
    return g, [mate_x, mate_q + mate_part] + contacts + grads


def tail(g, others, statics, pick, even, pieces):
    part, _ = contact_terms(g[:, LOW:HIGH], others[1], statics, False)
    glued = [
        penalty * (face - fine_dot(side, matrix))
        for face, side, matrix in zip(faces_of(g, even), others[4:], pick)
    ]
    zeros = jnp.zeros((CASES, M - HIGH), f32)
    image = whole_dot(g, pieces)
    image = image + jnp.concatenate(placed(*glued, even) + [part, zeros], axis=1)
    norm = jnp.sum(g * g, axis=1, keepdims=True)
    curve = jnp.sum(g * image, axis=1, keepdims=True)
    lane = lax.broadcasted_iota(jnp.int32, (CASES, BLK), 1)
    row = lax.broadcasted_iota(jnp.int32, (CASES, BLK), 0)
    spread = jnp.where(lane == row, norm, 0.0) + jnp.where(lane == row + CASES, curve, 0.0)
    return image, jnp.sum(spread, axis=0, keepdims=True)


def step_of(sums):
    total = jnp.sum(sums, axis=0, keepdims=True)
    lane = lax.broadcasted_iota(jnp.int32, (CASES, BLK), 1)
    row = lax.broadcasted_iota(jnp.int32, (CASES, BLK), 0)
    norm = jnp.sum(jnp.where(lane == row, total, 0.0), axis=1, keepdims=True)
    curve = jnp.sum(jnp.where(lane == row + CASES, total, 0.0), axis=1, keepdims=True)
    return norm, norm / curve


def moved_by(x, step, g):
    moved = x - step * g
    return jnp.maximum(moved, 0.0), jnp.maximum(-moved, 0.0)


def all_moved(x, step, g):
    moved = x - step * g
    contact = moved[:, LOW:HIGH]
    x = jnp.concatenate([moved[:, :LOW], jnp.maximum(contact, 0.0), moved[:, HIGH:]], axis=1)
    return x, jnp.maximum(-contact, 0.0)


def advance(sums, own, others, mate, near, far, statics, rows, coarse):
    _, step = step_of(sums)
    x, g, image = own
    x, lift = all_moved(x, step, g)
    mate_x, mate_g, near_x, far_x, near_face, far_face = others
    mate_kernel, near_kernel, far_kernel = coarse
    mate_x, mate_lift = moved_by(mate_x, step, mate_g)
    near_x, near_lift = moved_by(near_x, step, near[:, BLK:])
    far_x, far_lift = moved_by(far_x, step, far[:, BLK:])
    part, mate_part = contact_terms(lift, mate_lift, statics, True)
    mate_g = mate_g - step * mate + symmetric_dot(mate_lift, *mate_kernel) + mate_part
    near_face = near_face - step * near[:, :BLK] + fine_dot(near_lift, near_kernel[...])
    far_face = far_face - step * far[:, :BLK] + fine_dot(far_lift, far_kernel[...])
    lifted = whole_dot(lift, rows)
    g = g - step * image + lifted
    g = jnp.concatenate([g[:, :LOW], g[:, LOW:HIGH] + part, g[:, HIGH:]], axis=1)
    return x, g, [mate_x, mate_g, near_x, far_x, near_face, far_face]


CHUNK = 256
STARTS = (LOW, LOW + CHUNK) + (0,) + tuple(range(HIGH, M, CHUNK))


def whole_copy(dual_hbm, dual_ref, sems, starts=None):
    copies = []
    for index, start in enumerate(starts or STARTS):
        span = pl.ds(start, CHUNK)
        copies.append(
            pltpu.make_async_copy(dual_hbm.at[span], dual_ref.at[span], sems.at[index])
        )
    for copy in copies:
        copy.start()

    def piece(index, wait):
        def read():
            if wait:
                copies[index].wait()
            return dual_ref[pl.ds(STARTS[index], CHUNK), :]

        return (STARTS[index], CHUNK, read)

    return piece


TABLE = 2 * CASES
SLOTS = TABLE + CASES
UPPER = SLOTS + BLK
UNIT = BLK // 4
HALF = 5 * UNIT
PACKED = UPPER + HALF
HALVES = (
    ((0, 0), (0, 1), (0, 2), (0, 3), (1, 1)),
    ((1, 2), (1, 3), (2, 2), (2, 3), (3, 3)),
)
SIDE = 6 * CASES


def is_even():
    return lax.rem(lax.axis_index("sub"), 2) == 0


def halves(block):
    high = block.astype(bf16)
    return high, (block - high.astype(f32)).astype(bf16)


def is_odd_case():
    return lax.rem(lax.axis_index("case"), 2) == 1


def store_half(packed, dual_ref):
    odd = is_odd_case()
    for n in range(5):
        for k in range(4):
            pair = []
            for half in HALVES:
                row, lane = (LOW + BLK * place for place in half[n])
                pair.append(dual_ref[row + k * UNIT : row + (k + 1) * UNIT, lane : lane + BLK])
            rows = slice(UPPER + n * UNIT, UPPER + (n + 1) * UNIT)
            packed[rows, k * BLK : (k + 1) * BLK] = jnp.where(odd, pair[1], pair[0])


def symmetric_dot(value, mine, other):
    odd = is_odd_case()
    pieces = jnp.where(odd, other, mine), jnp.where(odd, mine, other)
    blocks = {}
    for half, piece in zip(HALVES, pieces):
        for n, key in enumerate(half):
            blocks[key] = jnp.concatenate(split(piece[n * UNIT : (n + 1) * UNIT]), axis=0)
    both = [jnp.concatenate(halves(block), axis=0) for block in split(value)]
    outs = []
    for j in range(4):
        total = None
        for i in range(4):
            part = dot(both[i], blocks[min(i, j), max(i, j)], i > j)
            total = part if total is None else total + part
        outs.append(total[:CASES] + total[CASES:])
    return jnp.concatenate(outs, axis=1)


def prepare_kernel(*refs):
    ids, count, x_ref, right_ref, mortar, dual_hbm = refs[:6]
    q_ref, packed, near_ref, far_ref, dual_ref, sems = refs[6:]
    piece = whole_copy(dual_hbm, dual_ref, sems)
    even = is_even()
    for k in range(4):
        packed[SLOTS:UPPER, k * BLK : (k + 1) * BLK] = mortar[k * BLK : (k + 1) * BLK, :]
    table = slot_table(ids, count).astype(bf16)
    packed[TABLE:SLOTS, :] = jnp.concatenate([table] * 4, axis=1)
    x = x_ref[...]
    q = whole_dot(x, [piece(k, True) for k in range(len(STARTS))]) - right_ref[...]
    q_ref[...] = q
    store_half(packed, dual_ref)
    packed[:CASES, :] = x[:, LOW:HIGH].astype(bf16)
    packed[CASES:TABLE, :] = q[:, LOW:HIGH].astype(bf16)
    contacts = split(x[:, LOW:HIGH])
    both = [(near_ref,), (far_ref,)]
    for (ref,), face, grad in zip(both, faces_of(x, even), faces_of(q, even)):
        for k, block in enumerate([face, grad] + contacts):
            ref[k * CASES : (k + 1) * CASES, :] = block.astype(bf16)
    first, second = dual_ref[LOW:HIGH, :BLK], dual_ref[LOW:HIGH, BLK:LOW]
    near_ref[SIDE:, :] = chosen(even, second, first)
    far_ref[SIDE:, :] = chosen(even, first, second)


def statics_of(ids, count, mortar, packed):
    own = [mortar[k * BLK : (k + 1) * BLK, :] for k in range(4)]
    mate = [packed[SLOTS:UPPER, k * BLK : (k + 1) * BLK] for k in range(4)]
    mate_table = packed[TABLE:SLOTS, :BLK].astype(f32)
    return slots(slot_table(ids, count)), own, slots(mate_table), mate


def side_values(ref):
    parts = [ref[k * CASES : (k + 1) * CASES, :].astype(f32) for k in range(6)]
    return jnp.concatenate(parts, axis=1)


def emit(outs, x, g, image, row, others):
    own_out, others_out, row_out, mate_out, near_out, far_out = outs
    row_out[...] = jnp.broadcast_to(row, row_out.shape)
    own_out[:, :M] = x
    own_out[:, M : 2 * M] = g
    own_out[:, 2 * M :] = image
    others_out[...] = jnp.concatenate(others, axis=1)
    mate_out[...] = image[:, LOW:HIGH]
    contact = g[:, LOW:HIGH]
    for ref, face in zip((near_out, far_out), faces_of(image, is_even())):
        ref[:, :BLK] = face
        ref[:, BLK:] = contact


def begin_kernel(*refs):
    ids, count, x_ref, q_ref, near, far, mortar, packed, match, dual_hbm = refs[:10]
    outs, (dual_ref, sems) = refs[10:16], refs[16:]
    piece = whole_copy(dual_hbm, dual_ref, sems)
    even = is_even()
    statics = statics_of(ids, count, mortar, packed)
    pick = picks(match[...], even)
    x = x_ref[...]
    mate = packed[:CASES, :].astype(f32), packed[CASES:TABLE, :].astype(f32)
    sides = side_values(near), side_values(far)
    g, others = begin(x, q_ref[...], mate, *sides, statics, pick, even)
    pieces = [piece(k, True) for k in range(len(STARTS))]
    image, row = tail(g, others, statics, pick, even, pieces)
    emit(outs, x, g, image, row, others)


WIDTHS = (CONTACT, CONTACT, CONTACT, CONTACT, BLK, BLK)


def advanced(refs, piece):
    ids, count, sums, own, others, mate, near, far, mortar, packed, _ = refs[:11]
    near_kernel, far_kernel, other_half = refs[11:14]
    mate_kernel = packed[UPPER:, :], other_half[...]
    statics = statics_of(ids, count, mortar, packed)
    offsets = [sum(WIDTHS[:k]) for k in range(len(WIDTHS))]
    lift_rows = [(k * CHUNK, CHUNK, piece(k, True)[2]) for k in range(2)]
    x, g, others = advance(
        sums[...],
        (own[:, :M], own[:, M : 2 * M], own[:, 2 * M :]),
        [others[:, start : start + size] for start, size in zip(offsets, WIDTHS)],
        mate[...],
        near[...],
        far[...],
        statics,
        lift_rows,
        (mate_kernel, near_kernel.at[SIDE:], far_kernel.at[SIDE:]),
    )
    return x, g, others, statics


def advance_kernel(*refs):
    dual_hbm, outs, (dual_ref, sems) = refs[14], refs[15:21], refs[21:]
    piece = whole_copy(dual_hbm, dual_ref, sems)
    even = is_even()
    x, g, others, statics = advanced(refs[:14], piece)
    pick = picks(refs[10][...], even)
    pieces = [piece(k, k >= 2) for k in range(len(STARTS))]
    image, row = tail(g, others, statics, pick, even, pieces)
    emit(outs, x, g, image, row, others)


def last_advance_kernel(*refs):
    dual_hbm, (own_out, others_out, row_out), (dual_ref, sems) = refs[14], refs[15:18], refs[18:]
    piece = whole_copy(dual_hbm, dual_ref, sems, STARTS[:2])
    x, g, others, _ = advanced(refs[:14], piece)
    own_out[:, :M] = x
    own_out[:, M:] = g
    others_out[...] = jnp.concatenate([others[1], others[4], others[5]], axis=1)
    total = jnp.sum(jnp.sum(g * g, axis=1, keepdims=True), axis=0, keepdims=True)
    row_out[...] = jnp.broadcast_to(total, row_out.shape)


def last_tail_kernel(*refs):
    ids, count, own, others, mortar, packed, match, dual_hbm = refs[:8]
    row_out, dual_ref, sems = refs[8:]
    piece = whole_copy(dual_hbm, dual_ref, sems)
    even = is_even()
    statics = statics_of(ids, count, mortar, packed)
    pick = picks(match[...], even)
    others = [
        None,
        others[:, :CONTACT],
        None,
        None,
        others[:, CONTACT : CONTACT + BLK],
        others[:, CONTACT + BLK :],
    ]
    pieces = [piece(k, True) for k in range(len(STARTS))]
    _, row = tail(own[:, M:], others, statics, pick, even, pieces)
    row_out[...] = jnp.broadcast_to(row, row_out.shape)


def finish_kernel(sums, own, x_out, norm_out):
    rows = sums[...]
    _, step = step_of(rows)
    x, _ = all_moved(own[:, :M], step, own[:, M : 2 * M])
    x_out[...] = x
    total = jnp.sum(rows, axis=0, keepdims=True)[:, 2 * CASES : 2 * CASES + 1]
    norm_out[...] = jnp.broadcast_to(jnp.sqrt(total), norm_out.shape)


VMEM_SPEC = pl.BlockSpec(memory_space=pltpu.VMEM)
SMEM_SPEC = pl.BlockSpec(memory_space=pltpu.SMEM)
HBM_SPEC = pl.BlockSpec(memory_space=pltpu.HBM)


def call(kernel, specs, shapes, operands, scratch=True, grant=52):
    scratch_shapes = [pltpu.VMEM((M, M), bf16), pltpu.SemaphoreType.DMA((len(STARTS),))] if scratch else []
    return pl.pallas_call(
        kernel,
        in_specs=specs,
        out_specs=[VMEM_SPEC] * len(shapes),
        out_shape=[jax.ShapeDtypeStruct(shape, kind) for shape, kind in shapes],
        scratch_shapes=scratch_shapes,
        compiler_params=pltpu.CompilerParams(vmem_limit_bytes=grant << 20),
    )(*operands)


def swapped(value, other):
    devices = lax.axis_size("sub")
    return lax.ppermute(value, "sub", [(i, other(i) % devices) for i in range(devices)])


def with_mate(value):
    half_axis = lax.axis_size("sub") // 2
    return swapped(value, lambda i: i + half_axis)


def with_near(value):
    return swapped(value, lambda i: i ^ 1)


def with_far(value):
    return swapped(value, lambda i: i + 1 if i % 2 else i - 1)


def with_case(value, bit):
    cases = lax.axis_size("case")
    return lax.ppermute(value, "case", [(i, i ^ bit) for i in range(cases)])


def spread_sums(copies, axis):
    devices = lax.axis_size(axis)
    rows = lax.all_to_all(copies.reshape(devices, 1, BLK), axis, 0, 0)
    return rows.reshape(devices, BLK)


def on_device(multipliers, right_side, dual_ops, glue_match, mortar, contact_ids, contact_count):
    devices = lax.axis_size("sub")
    mortar = mortar.reshape(CONTACT, BLK)
    match = glue_match[0]
    scalars = [SMEM_SPEC, SMEM_SPEC]

    q, packed, to_near, to_far = call(
        prepare_kernel,
        scalars + [VMEM_SPEC] * 3 + [HBM_SPEC],
        [
            ((CASES, M), f32),
            ((PACKED, CONTACT), bf16),
            ((SIDE + CONTACT, BLK), bf16),
            ((SIDE + CONTACT, BLK), bf16),
        ],
        (contact_ids, contact_count, multipliers, right_side, mortar, dual_ops),
        grant=PREPARE_GRANT,
    )
    packed = with_mate(packed)
    near = near_kernel = with_near(to_near)
    far = far_kernel = with_far(to_far)

    shapes = [
        ((CASES, 3 * M), f32),
        ((CASES, sum(WIDTHS)), f32),
        ((devices, BLK), f32),
        ((CASES, CONTACT), f32),
        ((CASES, BLK + CONTACT), f32),
        ((CASES, BLK + CONTACT), f32),
    ]
    own, others, copies, to_mate, to_near, to_far = call(
        begin_kernel,
        scalars + [VMEM_SPEC] * 7 + [HBM_SPEC],
        shapes,
        (
            contact_ids, contact_count, multipliers, q, near, far, mortar, packed, match,
            dual_ops,
        ),
    )
    for iteration in range(1, ITERS):
        sums = spread_sums(copies, "sub")
        mate = with_mate(to_mate)
        far = with_far(to_far)
        near = with_near(to_near)
        if iteration == 1:
            other_half = with_case(packed[UPPER:], 1)
        operands = (
            contact_ids, contact_count, sums, own, others, mate, near, far, mortar, packed,
            match, near_kernel, far_kernel, other_half, dual_ops,
        )
        if iteration < ITERS - 1:
            own, others, copies, to_mate, to_near, to_far = call(
                advance_kernel,
                scalars + [VMEM_SPEC] * 12 + [HBM_SPEC],
                shapes,
                operands,
            )
    cases = lax.axis_size("case")
    own, others, norms = call(
        last_advance_kernel,
        scalars + [VMEM_SPEC] * 12 + [HBM_SPEC],
        [
            ((CASES, 2 * M), f32),
            ((CASES, CONTACT + 2 * BLK), f32),
            ((cases, BLK), f32),
        ],
        operands,
    )
    norms = spread_sums(norms, "case")
    (copies,) = call(
        last_tail_kernel,
        scalars + [VMEM_SPEC] * 5 + [HBM_SPEC],
        [((devices, BLK), f32)],
        (contact_ids, contact_count, own, others, mortar, packed, match, dual_ops),
    )
    lane = lax.broadcasted_iota(jnp.int32, (1, BLK), 1)
    norm_row = jnp.where(lane == 2 * CASES, jnp.sum(norms, axis=0, keepdims=True), 0.0)
    sums = spread_sums(copies + norm_row, "sub")
    x, norm = call(
        finish_kernel,
        [VMEM_SPEC, VMEM_SPEC],
        [((CASES, M), f32), ((1, BLK), f32)],
        (sums, own),
        scratch=False,
        grant=16,
    )
    return (x, norm[0, :1])


PREPARE_GRANT = 60


def solution(mesh):
    in_specs = (
        P("case", "sub"),
        P("case", "sub"),
        P("sub", None),
        P("sub", None, None),
        P("sub", None, None, None),
        P("sub", None),
        P("sub"),
    )
    out_specs = (P("case", "sub"), P())
    return jax.shard_map(
        on_device, mesh=mesh, in_specs=in_specs, out_specs=out_specs, check_vma=False
    )
```

```python
import jax
import jax.numpy as jnp
from jax import lax
from jax.experimental import pallas as pl
from jax.experimental.pallas import tpu as pltpu
from jax.sharding import PartitionSpec as P

M = 1536
BLK = 128
ITERS = 4
CASES = 16
LOW, HIGH = 2 * BLK, 6 * BLK
CONTACT = HIGH - LOW

penalty = 0.5
f32, bf16 = jnp.float32, jnp.bfloat16


def dot(value, matrix, transposed=False):
    contract = 1 if transposed else 0
    return lax.dot_general(
        value, matrix, (((1,), (contract,)), ((), ())), preferred_element_type=f32
    )


def fine_dot(value, matrix, transposed=False):
    high = value.astype(bf16)
    low = (value - high.astype(f32)).astype(bf16)
    both = dot(jnp.concatenate([high, low], axis=0), matrix, transposed)
    return both[:CASES] + both[CASES:]


def split(value):
    return [value[:, k * BLK : (k + 1) * BLK] for k in range(value.shape[1] // BLK)]


def weighed(weights, values):
    total = weights[0] * values[0]
    for weight, value in zip(weights[1:], values[1:]):
        total = total + weight * value
    return total


def slots(meta):
    onehot = [[meta[:, 4 * k + b : 4 * k + b + 1] for b in range(4)] for k in range(4)]
    active = [meta[:, 16 + k : 17 + k] for k in range(4)]
    return onehot, active


def slot_table(ids, count):
    lane = lax.broadcasted_iota(jnp.int32, (CASES, BLK), 1)
    table = jnp.zeros((CASES, BLK), f32)
    for k in range(4):
        table = jnp.where(lane == ids[0, k] + 4 * k, 1.0, table)
        alive = jnp.where(count[0] > k, 1.0, 0.0).astype(f32)
        table = jnp.where(lane == 16 + k, alive, table)
    return table


def jump_of(slave, own, terms, mortar):
    onehot, active = terms
    return [
        (fine_dot(weighed(onehot[k], slave), mortar[k]) - own[k]) * active[k] for k in range(4)
    ]


def reply_of(jump, terms, mortar):
    onehot, _ = terms
    rows = [fine_dot(jump[k], mortar[k], True) for k in range(4)]
    return [weighed([onehot[k][b] for k in range(4)], rows) for b in range(4)]


def contact_terms(own, mate, statics, both):
    terms, mortar, mate_terms, mate_mortar = statics[:4]
    own, mate = split(own), split(mate)
    jump = jump_of(mate, own, terms, mortar)
    mate_jump = jump_of(own, mate, mate_terms, mate_mortar)
    part = [r - j for r, j in zip(reply_of(mate_jump, mate_terms, mate_mortar), jump)]
    if not both:
        return jnp.concatenate(part, axis=1), None
    mate_part = [r - j for r, j in zip(reply_of(jump, terms, mortar), mate_jump)]
    return jnp.concatenate(part, axis=1), jnp.concatenate(mate_part, axis=1)


def chosen(even, first, second):
    return jnp.where(even, first, second)


def picks(match, even):
    rows = lax.broadcasted_iota(jnp.int32, (BLK, BLK), 0)
    first, second = match[0:1, :], match[1:2, :]
    sides = (chosen(even, second, first), chosen(even, first, second))
    return [jnp.where(rows == side, 1.0, 0.0).astype(bf16) for side in sides]


def faces_of(value, even):
    first, second = value[:, :BLK], value[:, BLK:LOW]
    return chosen(even, second, first), chosen(even, first, second)


def placed(near, far, even):
    return [chosen(even, far, near), chosen(even, near, far)]


def whole_dot(value, pieces):
    high = value.astype(bf16)
    low = (value - high.astype(f32)).astype(bf16)
    both, total = jnp.concatenate([high, low], axis=0), None
    for start, size, piece in pieces:
        part = dot(both[:, start : start + size], piece())
        total = part if total is None else total + part
    return total[:CASES] + total[CASES:]


def begin(x, q, mate, near, far, statics, pick, even):
    mate_x, mate_q = mate
    part, mate_part = contact_terms(x[:, LOW:HIGH], mate_x, statics, True)
    own = faces_of(x, even)
    glued, grads, contacts = [], [], []
    for side, face, matrix in zip((near, far), own, pick):
        side_x, side_q, contact = side[:, :BLK], side[:, BLK : 2 * BLK], side[:, 2 * BLK :]
        glued.append(penalty * (face - fine_dot(side_x, matrix)))
        grads.append(side_q + penalty * (side_x - fine_dot(face, matrix, True)))
        contacts.append(contact)
    faces = jnp.concatenate(placed(*glued, even), axis=1)
    g = jnp.concatenate(
        [q[:, :LOW] + faces, q[:, LOW:HIGH] + part, q[:, HIGH:]],
        axis=1,
    )
    return g, [mate_x, mate_q + mate_part] + contacts + grads


def tail(g, others, statics, pick, even, pieces):
    part, _ = contact_terms(g[:, LOW:HIGH], others[1], statics, False)
    glued = [
        penalty * (face - fine_dot(side, matrix))
        for face, side, matrix in zip(faces_of(g, even), others[4:], pick)
    ]
    zeros = jnp.zeros((CASES, M - HIGH), f32)
    image = whole_dot(g, pieces)
    image = image + jnp.concatenate(placed(*glued, even) + [part, zeros], axis=1)
    norm = jnp.sum(g * g, axis=1, keepdims=True)
    curve = jnp.sum(g * image, axis=1, keepdims=True)
    lane = lax.broadcasted_iota(jnp.int32, (CASES, BLK), 1)
    row = lax.broadcasted_iota(jnp.int32, (CASES, BLK), 0)
    spread = jnp.where(lane == row, norm, 0.0) + jnp.where(lane == row + CASES, curve, 0.0)
    return image, jnp.sum(spread, axis=0, keepdims=True)


def step_of(sums):
    total = jnp.sum(sums, axis=0, keepdims=True)
    lane = lax.broadcasted_iota(jnp.int32, (CASES, BLK), 1)
    row = lax.broadcasted_iota(jnp.int32, (CASES, BLK), 0)
    norm = jnp.sum(jnp.where(lane == row, total, 0.0), axis=1, keepdims=True)
    curve = jnp.sum(jnp.where(lane == row + CASES, total, 0.0), axis=1, keepdims=True)
    return norm, norm / curve


def moved_by(x, step, g):
    moved = x - step * g
    return jnp.maximum(moved, 0.0), jnp.maximum(-moved, 0.0)


def all_moved(x, step, g):
    moved = x - step * g
    contact = moved[:, LOW:HIGH]
    x = jnp.concatenate([moved[:, :LOW], jnp.maximum(contact, 0.0), moved[:, HIGH:]], axis=1)
    return x, jnp.maximum(-contact, 0.0)


def advance(sums, own, others, mate, near, far, statics, rows, coarse):
    _, step = step_of(sums)
    x, g, image = own
    x, lift = all_moved(x, step, g)
    mate_x, mate_g, near_x, far_x, near_face, far_face = others
    mate_kernel, near_kernel, far_kernel = coarse
    mate_x, mate_lift = moved_by(mate_x, step, mate_g)
    near_x, near_lift = moved_by(near_x, step, near[:, BLK:])
    far_x, far_lift = moved_by(far_x, step, far[:, BLK:])
    part, mate_part = contact_terms(lift, mate_lift, statics, True)
    mate_g = mate_g - step * mate + symmetric_dot(mate_lift, *mate_kernel) + mate_part
    near_face = near_face - step * near[:, :BLK] + fine_dot(near_lift, near_kernel[...])
    far_face = far_face - step * far[:, :BLK] + fine_dot(far_lift, far_kernel[...])
    lifted = whole_dot(lift, rows)
    g = g - step * image + lifted
    g = jnp.concatenate([g[:, :LOW], g[:, LOW:HIGH] + part, g[:, HIGH:]], axis=1)
    return x, g, [mate_x, mate_g, near_x, far_x, near_face, far_face]


CHUNK = 256
STARTS = (LOW, LOW + CHUNK) + (0,) + tuple(range(HIGH, M, CHUNK))


def whole_copy(dual_hbm, dual_ref, sems, starts=None):
    copies = []
    for index, start in enumerate(starts or STARTS):
        span = pl.ds(start, CHUNK)
        copies.append(
            pltpu.make_async_copy(dual_hbm.at[span], dual_ref.at[span], sems.at[index])
        )
    for copy in copies:
        copy.start()

    def piece(index, wait):
        def read():
            if wait:
                copies[index].wait()
            return dual_ref[pl.ds(STARTS[index], CHUNK), :]

        return (STARTS[index], CHUNK, read)

    return piece


TABLE = 0
SLOTS = TABLE + CASES
UPPER = SLOTS + BLK
UNIT = BLK // 4
HALF = 5 * UNIT
PACKED = UPPER + HALF
HALVES = (
    ((0, 0), (0, 1), (0, 2), (0, 3), (1, 1)),
    ((1, 2), (1, 3), (2, 2), (2, 3), (3, 3)),
)
SIDE = 6 * CASES


def is_even():
    return lax.rem(lax.axis_index("sub"), 2) == 0


def halves(block):
    high = block.astype(bf16)
    return high, (block - high.astype(f32)).astype(bf16)


def is_odd_case():
    return lax.rem(lax.axis_index("case"), 2) == 1


def store_half(packed, block_ref):
    odd = is_odd_case()
    for n in range(5):
        for k in range(4):
            pair = []
            for half in HALVES:
                row, lane = (BLK * place for place in half[n])
                pair.append(block_ref[row + k * UNIT : row + (k + 1) * UNIT, lane : lane + BLK])
            rows = slice(UPPER + n * UNIT, UPPER + (n + 1) * UNIT)
            packed[rows, k * BLK : (k + 1) * BLK] = jnp.where(odd, pair[1], pair[0])


def symmetric_dot(value, mine, other):
    odd = is_odd_case()
    pieces = jnp.where(odd, other, mine), jnp.where(odd, mine, other)
    blocks = {}
    for half, piece in zip(HALVES, pieces):
        for n, key in enumerate(half):
            blocks[key] = jnp.concatenate(split(piece[n * UNIT : (n + 1) * UNIT]), axis=0)
    both = [jnp.concatenate(halves(block), axis=0) for block in split(value)]
    outs = []
    for j in range(4):
        total = None
        for i in range(4):
            part = dot(both[i], blocks[min(i, j), max(i, j)], i > j)
            total = part if total is None else total + part
        outs.append(total[:CASES] + total[CASES:])
    return jnp.concatenate(outs, axis=1)


def pack_kernel(ids, count, mortar, dual_hbm, packed, block_ref, sem):
    contact = pl.ds(LOW, CONTACT)
    copy = pltpu.make_async_copy(dual_hbm.at[contact, contact], block_ref, sem)
    copy.start()
    for k in range(4):
        packed[SLOTS:UPPER, k * BLK : (k + 1) * BLK] = mortar[k * BLK : (k + 1) * BLK, :]
    table = slot_table(ids, count).astype(bf16)
    packed[TABLE:SLOTS, :] = jnp.concatenate([table] * 4, axis=1)
    copy.wait()
    store_half(packed, block_ref)


def prepare_kernel(*refs):
    x_ref, right_ref, dual_hbm, q_ref, first_ref, near_ref, far_ref, dual_ref, sems = refs
    piece = whole_copy(dual_hbm, dual_ref, sems)
    even = is_even()
    x = x_ref[...]
    q = whole_dot(x, [piece(k, True) for k in range(len(STARTS))]) - right_ref[...]
    q_ref[...] = q
    first_ref[:CASES, :] = x[:, LOW:HIGH].astype(bf16)
    first_ref[CASES:, :] = q[:, LOW:HIGH].astype(bf16)
    contacts = split(x[:, LOW:HIGH])
    both = [(near_ref,), (far_ref,)]
    for (ref,), face, grad in zip(both, faces_of(x, even), faces_of(q, even)):
        for k, block in enumerate([face, grad] + contacts):
            ref[k * CASES : (k + 1) * CASES, :] = block.astype(bf16)
    first, second = dual_ref[LOW:HIGH, :BLK], dual_ref[LOW:HIGH, BLK:LOW]
    near_ref[SIDE:, :] = chosen(even, second, first)
    far_ref[SIDE:, :] = chosen(even, first, second)


def statics_of(ids, count, mortar, packed):
    own = [mortar[k * BLK : (k + 1) * BLK, :] for k in range(4)]
    mate = [packed[SLOTS:UPPER, k * BLK : (k + 1) * BLK] for k in range(4)]
    mate_table = packed[TABLE:SLOTS, :BLK].astype(f32)
    return slots(slot_table(ids, count)), own, slots(mate_table), mate


def side_values(ref):
    parts = [ref[k * CASES : (k + 1) * CASES, :].astype(f32) for k in range(6)]
    return jnp.concatenate(parts, axis=1)


def emit(outs, x, g, image, row, others):
    own_out, others_out, row_out, mate_out, near_out, far_out = outs
    row_out[...] = jnp.broadcast_to(row, row_out.shape)
    own_out[:, :M] = x
    own_out[:, M : 2 * M] = g
    own_out[:, 2 * M :] = image
    others_out[...] = jnp.concatenate(others, axis=1)
    mate_out[...] = image[:, LOW:HIGH]
    contact = g[:, LOW:HIGH]
    for ref, face in zip((near_out, far_out), faces_of(image, is_even())):
        ref[:, :BLK] = face
        ref[:, BLK:] = contact


def begin_kernel(*refs):
    ids, count, x_ref, q_ref, first, near, far, mortar, packed, match, dual_hbm = refs[:11]
    outs, (dual_ref, sems) = refs[11:17], refs[17:]
    piece = whole_copy(dual_hbm, dual_ref, sems)
    even = is_even()
    statics = statics_of(ids, count, mortar, packed)
    pick = picks(match[...], even)
    x = x_ref[...]
    mate = first[:CASES, :].astype(f32), first[CASES:, :].astype(f32)
    sides = side_values(near), side_values(far)
    g, others = begin(x, q_ref[...], mate, *sides, statics, pick, even)
    pieces = [piece(k, True) for k in range(len(STARTS))]
    image, row = tail(g, others, statics, pick, even, pieces)
    emit(outs, x, g, image, row, others)


WIDTHS = (CONTACT, CONTACT, CONTACT, CONTACT, BLK, BLK)


def advanced(refs, piece):
    ids, count, sums, own, others, mate, near, far, mortar, packed, _ = refs[:11]
    near_kernel, far_kernel, other_half = refs[11:14]
    mate_kernel = packed[UPPER:, :], other_half[...]
    statics = statics_of(ids, count, mortar, packed)
    offsets = [sum(WIDTHS[:k]) for k in range(len(WIDTHS))]
    lift_rows = [(k * CHUNK, CHUNK, piece(k, True)[2]) for k in range(2)]
    x, g, others = advance(
        sums[...],
        (own[:, :M], own[:, M : 2 * M], own[:, 2 * M :]),
        [others[:, start : start + size] for start, size in zip(offsets, WIDTHS)],
        mate[...],
        near[...],
        far[...],
        statics,
        lift_rows,
        (mate_kernel, near_kernel.at[SIDE:], far_kernel.at[SIDE:]),
    )
    return x, g, others, statics


def advance_kernel(*refs):
    dual_hbm, outs, (dual_ref, sems) = refs[14], refs[15:21], refs[21:]
    piece = whole_copy(dual_hbm, dual_ref, sems)
    even = is_even()
    x, g, others, statics = advanced(refs[:14], piece)
    pick = picks(refs[10][...], even)
    pieces = [piece(k, k >= 2) for k in range(len(STARTS))]
    image, row = tail(g, others, statics, pick, even, pieces)
    emit(outs, x, g, image, row, others)


def last_advance_kernel(*refs):
    dual_hbm, (own_out, others_out, row_out), (dual_ref, sems) = refs[14], refs[15:18], refs[18:]
    piece = whole_copy(dual_hbm, dual_ref, sems, STARTS[:2])
    x, g, others, _ = advanced(refs[:14], piece)
    own_out[:, :M] = x
    own_out[:, M:] = g
    others_out[...] = jnp.concatenate([others[1], others[4], others[5]], axis=1)
    total = jnp.sum(jnp.sum(g * g, axis=1, keepdims=True), axis=0, keepdims=True)
    row_out[...] = jnp.broadcast_to(total, row_out.shape)


def last_tail_kernel(*refs):
    ids, count, own, others, mortar, packed, match, dual_hbm = refs[:8]
    row_out, dual_ref, sems = refs[8:]
    piece = whole_copy(dual_hbm, dual_ref, sems)
    even = is_even()
    statics = statics_of(ids, count, mortar, packed)
    pick = picks(match[...], even)
    others = [
        None,
        others[:, :CONTACT],
        None,
        None,
        others[:, CONTACT : CONTACT + BLK],
        others[:, CONTACT + BLK :],
    ]
    pieces = [piece(k, True) for k in range(len(STARTS))]
    _, row = tail(own[:, M:], others, statics, pick, even, pieces)
    row_out[...] = jnp.broadcast_to(row, row_out.shape)


def finish_kernel(sums, own, x_out, norm_out):
    rows = sums[...]
    _, step = step_of(rows)
    x, _ = all_moved(own[:, :M], step, own[:, M : 2 * M])
    x_out[...] = x
    total = jnp.sum(rows, axis=0, keepdims=True)[:, 2 * CASES : 2 * CASES + 1]
    norm_out[...] = jnp.broadcast_to(jnp.sqrt(total), norm_out.shape)


VMEM_SPEC = pl.BlockSpec(memory_space=pltpu.VMEM)
SMEM_SPEC = pl.BlockSpec(memory_space=pltpu.SMEM)
HBM_SPEC = pl.BlockSpec(memory_space=pltpu.HBM)


WHOLE = [pltpu.VMEM((M, M), bf16), pltpu.SemaphoreType.DMA((len(STARTS),))]
BLOCK = [pltpu.VMEM((CONTACT, CONTACT), bf16), pltpu.SemaphoreType.DMA]


def call(kernel, specs, shapes, operands, scratch=WHOLE, grant=52):
    return pl.pallas_call(
        kernel,
        in_specs=specs,
        out_specs=[VMEM_SPEC] * len(shapes),
        out_shape=[jax.ShapeDtypeStruct(shape, kind) for shape, kind in shapes],
        scratch_shapes=scratch,
        compiler_params=pltpu.CompilerParams(vmem_limit_bytes=grant << 20),
    )(*operands)


def swapped(value, other):
    devices = lax.axis_size("sub")
    return lax.ppermute(value, "sub", [(i, other(i) % devices) for i in range(devices)])


def with_mate(value):
    half_axis = lax.axis_size("sub") // 2
    return swapped(value, lambda i: i + half_axis)


def with_near(value):
    return swapped(value, lambda i: i ^ 1)


def with_far(value):
    return swapped(value, lambda i: i + 1 if i % 2 else i - 1)


def with_case(value, bit):
    cases = lax.axis_size("case")
    return lax.ppermute(value, "case", [(i, i ^ bit) for i in range(cases)])


def spread_sums(copies, axis):
    devices = lax.axis_size(axis)
    rows = lax.all_to_all(copies.reshape(devices, 1, BLK), axis, 0, 0)
    return rows.reshape(devices, BLK)


def on_device(multipliers, right_side, dual_ops, glue_match, mortar, contact_ids, contact_count):
    devices = lax.axis_size("sub")
    mortar = mortar.reshape(CONTACT, BLK)
    match = glue_match[0]
    scalars = [SMEM_SPEC, SMEM_SPEC]

    (packed,) = call(
        pack_kernel,
        scalars + [VMEM_SPEC, HBM_SPEC],
        [((PACKED, CONTACT), bf16)],
        (contact_ids, contact_count, mortar, dual_ops),
        scratch=BLOCK,
        grant=PREPARE_GRANT,
    )
    packed = with_mate(packed)
    q, first, to_near, to_far = call(
        prepare_kernel,
        [VMEM_SPEC] * 2 + [HBM_SPEC],
        [
            ((CASES, M), f32),
            ((2 * CASES, CONTACT), bf16),
            ((SIDE + CONTACT, BLK), bf16),
            ((SIDE + CONTACT, BLK), bf16),
        ],
        (multipliers, right_side, dual_ops),
        grant=PREPARE_GRANT,
    )
    first = with_mate(first)
    near = near_kernel = with_near(to_near)
    far = far_kernel = with_far(to_far)

    shapes = [
        ((CASES, 3 * M), f32),
        ((CASES, sum(WIDTHS)), f32),
        ((devices, BLK), f32),
        ((CASES, CONTACT), f32),
        ((CASES, BLK + CONTACT), f32),
        ((CASES, BLK + CONTACT), f32),
    ]
    own, others, copies, to_mate, to_near, to_far = call(
        begin_kernel,
        scalars + [VMEM_SPEC] * 8 + [HBM_SPEC],
        shapes,
        (
            contact_ids, contact_count, multipliers, q, first, near, far, mortar, packed,
            match, dual_ops,
        ),
    )
    for iteration in range(1, ITERS):
        sums = spread_sums(copies, "sub")
        mate = with_mate(to_mate)
        far = with_far(to_far)
        near = with_near(to_near)
        if iteration == 1:
            other_half = with_case(packed[UPPER:], 1)
        operands = (
            contact_ids, contact_count, sums, own, others, mate, near, far, mortar, packed,
            match, near_kernel, far_kernel, other_half, dual_ops,
        )
        if iteration < ITERS - 1:
            own, others, copies, to_mate, to_near, to_far = call(
                advance_kernel,
                scalars + [VMEM_SPEC] * 12 + [HBM_SPEC],
                shapes,
                operands,
            )
    cases = lax.axis_size("case")
    own, others, norms = call(
        last_advance_kernel,
        scalars + [VMEM_SPEC] * 12 + [HBM_SPEC],
        [
            ((CASES, 2 * M), f32),
            ((CASES, CONTACT + 2 * BLK), f32),
            ((cases, BLK), f32),
        ],
        operands,
    )
    norms = spread_sums(norms, "case")
    (copies,) = call(
        last_tail_kernel,
        scalars + [VMEM_SPEC] * 5 + [HBM_SPEC],
        [((devices, BLK), f32)],
        (contact_ids, contact_count, own, others, mortar, packed, match, dual_ops),
    )
    lane = lax.broadcasted_iota(jnp.int32, (1, BLK), 1)
    norm_row = jnp.where(lane == 2 * CASES, jnp.sum(norms, axis=0, keepdims=True), 0.0)
    sums = spread_sums(copies + norm_row, "sub")
    x, norm = call(
        finish_kernel,
        [VMEM_SPEC, VMEM_SPEC],
        [((CASES, M), f32), ((1, BLK), f32)],
        (sums, own),
        scratch=[],
        grant=16,
    )
    return (x, norm[0, :1])


PREPARE_GRANT = 60


def solution(mesh):
    in_specs = (
        P("case", "sub"),
        P("case", "sub"),
        P("sub", None),
        P("sub", None, None),
        P("sub", None, None, None),
        P("sub", None),
        P("sub"),
    )
    out_specs = (P("case", "sub"), P())
    return jax.shard_map(
        on_device, mesh=mesh, in_specs=in_specs, out_specs=out_specs, check_vma=False
    )
```

```python
import jax
import jax.numpy as jnp
from jax import lax
from jax.experimental import pallas as pl
from jax.experimental.pallas import tpu as pltpu
from jax.sharding import PartitionSpec as P

M = 1536
BLK = 128
ITERS = 4
CASES = 16
LOW, HIGH = 2 * BLK, 6 * BLK
CONTACT = HIGH - LOW

penalty = 0.5
f32, bf16 = jnp.float32, jnp.bfloat16


def dot(value, matrix, transposed=False):
    contract = 1 if transposed else 0
    return lax.dot_general(
        value, matrix, (((1,), (contract,)), ((), ())), preferred_element_type=f32
    )


def fine_dot(value, matrix, transposed=False):
    high = value.astype(bf16)
    low = (value - high.astype(f32)).astype(bf16)
    both = dot(jnp.concatenate([high, low], axis=0), matrix, transposed)
    return both[:CASES] + both[CASES:]


def split(value):
    return [value[:, k * BLK : (k + 1) * BLK] for k in range(value.shape[1] // BLK)]


def weighed(weights, values):
    total = weights[0] * values[0]
    for weight, value in zip(weights[1:], values[1:]):
        total = total + weight * value
    return total


def slots(meta):
    onehot = [[meta[:, 4 * k + b : 4 * k + b + 1] for b in range(4)] for k in range(4)]
    active = [meta[:, 16 + k : 17 + k] for k in range(4)]
    return onehot, active


def slot_table(ids, count):
    lane = lax.broadcasted_iota(jnp.int32, (CASES, BLK), 1)
    table = jnp.zeros((CASES, BLK), f32)
    for k in range(4):
        table = jnp.where(lane == ids[0, k] + 4 * k, 1.0, table)
        alive = jnp.where(count[0] > k, 1.0, 0.0).astype(f32)
        table = jnp.where(lane == 16 + k, alive, table)
    return table


def jump_of(slave, own, terms, mortar):
    onehot, active = terms
    return [
        (fine_dot(weighed(onehot[k], slave), mortar[k]) - own[k]) * active[k] for k in range(4)
    ]


def reply_of(jump, terms, mortar):
    onehot, _ = terms
    rows = [fine_dot(jump[k], mortar[k], True) for k in range(4)]
    return [weighed([onehot[k][b] for k in range(4)], rows) for b in range(4)]


def contact_terms(own, mate, statics, both):
    terms, mortar, mate_terms, mate_mortar = statics[:4]
    own, mate = split(own), split(mate)
    jump = jump_of(mate, own, terms, mortar)
    mate_jump = jump_of(own, mate, mate_terms, mate_mortar)
    part = [r - j for r, j in zip(reply_of(mate_jump, mate_terms, mate_mortar), jump)]
    if not both:
        return jnp.concatenate(part, axis=1), None
    mate_part = [r - j for r, j in zip(reply_of(jump, terms, mortar), mate_jump)]
    return jnp.concatenate(part, axis=1), jnp.concatenate(mate_part, axis=1)


def chosen(even, first, second):
    return jnp.where(even, first, second)


def picks(match, even):
    rows = lax.broadcasted_iota(jnp.int32, (BLK, BLK), 0)
    first, second = match[0:1, :], match[1:2, :]
    sides = (chosen(even, second, first), chosen(even, first, second))
    return [jnp.where(rows == side, 1.0, 0.0).astype(bf16) for side in sides]


def faces_of(value, even):
    first, second = value[:, :BLK], value[:, BLK:LOW]
    return chosen(even, second, first), chosen(even, first, second)


def placed(near, far, even):
    return [chosen(even, far, near), chosen(even, near, far)]


def whole_dot(value, pieces):
    high = value.astype(bf16)
    low = (value - high.astype(f32)).astype(bf16)
    both, total = jnp.concatenate([high, low], axis=0), None
    for start, size, piece in pieces:
        part = dot(both[:, start : start + size], piece())
        total = part if total is None else total + part
    return total[:CASES] + total[CASES:]


def begin(x, q, mate, near, far, statics, pick, even):
    mate_x, mate_q = mate
    part, mate_part = contact_terms(x[:, LOW:HIGH], mate_x, statics, True)
    own = faces_of(x, even)
    glued, grads, contacts = [], [], []
    for side, face, matrix in zip((near, far), own, pick):
        side_x, side_q, contact = side[:, :BLK], side[:, BLK : 2 * BLK], side[:, 2 * BLK :]
        glued.append(penalty * (face - fine_dot(side_x, matrix)))
        grads.append(side_q + penalty * (side_x - fine_dot(face, matrix, True)))
        contacts.append(contact)
    faces = jnp.concatenate(placed(*glued, even), axis=1)
    g = jnp.concatenate(
        [q[:, :LOW] + faces, q[:, LOW:HIGH] + part, q[:, HIGH:]],
        axis=1,
    )
    return g, [mate_x, mate_q + mate_part] + contacts + grads


def tail(g, others, statics, pick, even, pieces):
    part, _ = contact_terms(g[:, LOW:HIGH], others[1], statics, False)
    glued = [
        penalty * (face - fine_dot(side, matrix))
        for face, side, matrix in zip(faces_of(g, even), others[4:], pick)
    ]
    zeros = jnp.zeros((CASES, M - HIGH), f32)
    image = whole_dot(g, pieces)
    image = image + jnp.concatenate(placed(*glued, even) + [part, zeros], axis=1)
    norm = jnp.sum(g * g, axis=1, keepdims=True)
    curve = jnp.sum(g * image, axis=1, keepdims=True)
    lane = lax.broadcasted_iota(jnp.int32, (CASES, BLK), 1)
    row = lax.broadcasted_iota(jnp.int32, (CASES, BLK), 0)
    spread = jnp.where(lane == row, norm, 0.0) + jnp.where(lane == row + CASES, curve, 0.0)
    return image, jnp.sum(spread, axis=0, keepdims=True)


def step_of(sums):
    total = jnp.sum(sums, axis=0, keepdims=True)
    lane = lax.broadcasted_iota(jnp.int32, (CASES, BLK), 1)
    row = lax.broadcasted_iota(jnp.int32, (CASES, BLK), 0)
    norm = jnp.sum(jnp.where(lane == row, total, 0.0), axis=1, keepdims=True)
    curve = jnp.sum(jnp.where(lane == row + CASES, total, 0.0), axis=1, keepdims=True)
    return norm, norm / curve


def moved_by(x, step, g):
    moved = x - step * g
    return jnp.maximum(moved, 0.0), jnp.maximum(-moved, 0.0)


def all_moved(x, step, g):
    moved = x - step * g
    contact = moved[:, LOW:HIGH]
    x = jnp.concatenate([moved[:, :LOW], jnp.maximum(contact, 0.0), moved[:, HIGH:]], axis=1)
    return x, jnp.maximum(-contact, 0.0)


def advance(sums, own, others, mate, near, far, statics, rows, coarse):
    _, step = step_of(sums)
    x, g, image = own
    x, lift = all_moved(x, step, g)
    mate_x, mate_g, near_x, far_x, near_face, far_face = others
    mate_kernel, near_kernel, far_kernel = coarse
    mate_x, mate_lift = moved_by(mate_x, step, mate_g)
    near_x, near_lift = moved_by(near_x, step, near[:, BLK:])
    far_x, far_lift = moved_by(far_x, step, far[:, BLK:])
    part, mate_part = contact_terms(lift, mate_lift, statics, True)
    mate_g = mate_g - step * mate + symmetric_dot(mate_lift, *mate_kernel) + mate_part
    near_face = near_face - step * near[:, :BLK] + fine_dot(near_lift, near_kernel[...])
    far_face = far_face - step * far[:, :BLK] + fine_dot(far_lift, far_kernel[...])
    lifted = whole_dot(lift, rows)
    g = g - step * image + lifted
    g = jnp.concatenate([g[:, :LOW], g[:, LOW:HIGH] + part, g[:, HIGH:]], axis=1)
    return x, g, [mate_x, mate_g, near_x, far_x, near_face, far_face]


CHUNK = 256
STARTS = (LOW, LOW + CHUNK) + (0,) + tuple(range(HIGH, M, CHUNK))


def whole_copy(dual_hbm, dual_ref, sems, starts=None):
    copies = []
    for index, start in enumerate(starts or STARTS):
        span = pl.ds(start, CHUNK)
        copies.append(
            pltpu.make_async_copy(dual_hbm.at[span], dual_ref.at[span], sems.at[index])
        )
    for copy in copies:
        copy.start()

    def piece(index, wait):
        def read():
            if wait:
                copies[index].wait()
            return dual_ref[pl.ds(STARTS[index], CHUNK), :]

        return (STARTS[index], CHUNK, read)

    return piece


UNIT = BLK // 4
HALF = 5 * UNIT
HALVES = (
    ((0, 0), (0, 1), (0, 2), (0, 3), (1, 1)),
    ((1, 2), (1, 3), (2, 2), (2, 3), (3, 3)),
)
SIDE = 6 * CASES


def is_even():
    return lax.rem(lax.axis_index("sub"), 2) == 0


def halves(block):
    high = block.astype(bf16)
    return high, (block - high.astype(f32)).astype(bf16)


def is_odd_case():
    return lax.rem(lax.axis_index("case"), 2) == 1


def store_half(packed, block_ref):
    odd = is_odd_case()
    for n in range(5):
        for k in range(4):
            pair = []
            for half in HALVES:
                row, lane = (BLK * place for place in half[n])
                pair.append(block_ref[row + k * UNIT : row + (k + 1) * UNIT, lane : lane + BLK])
            rows = slice(n * UNIT, (n + 1) * UNIT)
            packed[rows, k * BLK : (k + 1) * BLK] = jnp.where(odd, pair[1], pair[0])


def symmetric_dot(value, mine, other):
    odd = is_odd_case()
    pieces = jnp.where(odd, other, mine), jnp.where(odd, mine, other)
    blocks = {}
    for half, piece in zip(HALVES, pieces):
        for n, key in enumerate(half):
            blocks[key] = jnp.concatenate(split(piece[n * UNIT : (n + 1) * UNIT]), axis=0)
    both = [jnp.concatenate(halves(block), axis=0) for block in split(value)]
    outs = []
    for j in range(4):
        total = None
        for i in range(4):
            part = dot(both[i], blocks[min(i, j), max(i, j)], i > j)
            total = part if total is None else total + part
        outs.append(total[:CASES] + total[CASES:])
    return jnp.concatenate(outs, axis=1)


def pack_kernel(dual_hbm, packed, block_ref, sem):
    contact = pl.ds(LOW, CONTACT)
    copy = pltpu.make_async_copy(dual_hbm.at[contact, contact], block_ref, sem)
    copy.start()
    copy.wait()
    store_half(packed, block_ref)


def prepare_kernel(*refs):
    ids, count, x_ref, right_ref, dual_hbm = refs[:5]
    q_ref, first_ref, near_ref, far_ref, dual_ref, sems = refs[5:]
    piece = whole_copy(dual_hbm, dual_ref, sems)
    even = is_even()
    x = x_ref[...]
    q = whole_dot(x, [piece(k, True) for k in range(len(STARTS))]) - right_ref[...]
    q_ref[...] = q
    first_ref[:CASES, :] = x[:, LOW:HIGH].astype(bf16)
    first_ref[CASES : 2 * CASES, :] = q[:, LOW:HIGH].astype(bf16)
    table = slot_table(ids, count).astype(bf16)
    first_ref[2 * CASES :, :] = jnp.concatenate([table] * 4, axis=1)
    contacts = split(x[:, LOW:HIGH])
    both = [(near_ref,), (far_ref,)]
    for (ref,), face, grad in zip(both, faces_of(x, even), faces_of(q, even)):
        for k, block in enumerate([face, grad] + contacts):
            ref[k * CASES : (k + 1) * CASES, :] = block.astype(bf16)
    first, second = dual_ref[LOW:HIGH, :BLK], dual_ref[LOW:HIGH, BLK:LOW]
    near_ref[SIDE:, :] = chosen(even, second, first)
    far_ref[SIDE:, :] = chosen(even, first, second)


def statics_of(ids, count, mortar, mate_mortar, first):
    own, mate = [
        [ref[k * BLK : (k + 1) * BLK, :] for k in range(4)] for ref in (mortar, mate_mortar)
    ]
    mate_table = first[2 * CASES :, :BLK].astype(f32)
    return slots(slot_table(ids, count)), own, slots(mate_table), mate


def side_values(ref):
    parts = [ref[k * CASES : (k + 1) * CASES, :].astype(f32) for k in range(6)]
    return jnp.concatenate(parts, axis=1)


def emit(outs, x, g, image, row, others):
    own_out, others_out, row_out, mate_out, near_out, far_out = outs
    row_out[...] = jnp.broadcast_to(row, row_out.shape)
    own_out[:, :M] = x
    own_out[:, M : 2 * M] = g
    own_out[:, 2 * M :] = image
    others_out[...] = jnp.concatenate(others, axis=1)
    mate_out[...] = image[:, LOW:HIGH]
    contact = g[:, LOW:HIGH]
    for ref, face in zip((near_out, far_out), faces_of(image, is_even())):
        ref[:, :BLK] = face
        ref[:, BLK:] = contact


def begin_kernel(*refs):
    ids, count, x_ref, q_ref, first, near, far, mortar, mate_mortar, match, dual_hbm = refs[:11]
    outs, (dual_ref, sems) = refs[11:17], refs[17:]
    piece = whole_copy(dual_hbm, dual_ref, sems)
    even = is_even()
    statics = statics_of(ids, count, mortar, mate_mortar, first)
    pick = picks(match[...], even)
    x = x_ref[...]
    mate = first[:CASES, :].astype(f32), first[CASES : 2 * CASES, :].astype(f32)
    sides = side_values(near), side_values(far)
    g, others = begin(x, q_ref[...], mate, *sides, statics, pick, even)
    pieces = [piece(k, True) for k in range(len(STARTS))]
    image, row = tail(g, others, statics, pick, even, pieces)
    emit(outs, x, g, image, row, others)


WIDTHS = (CONTACT, CONTACT, CONTACT, CONTACT, BLK, BLK)


def advanced(refs, piece):
    ids, count, sums, own, others, mate, near, far, mortar, mate_mortar, _ = refs[:11]
    first, near_kernel, far_kernel, half, other_half = refs[11:16]
    mate_kernel = half[...], other_half[...]
    statics = statics_of(ids, count, mortar, mate_mortar, first)
    offsets = [sum(WIDTHS[:k]) for k in range(len(WIDTHS))]
    lift_rows = [(k * CHUNK, CHUNK, piece(k, True)[2]) for k in range(2)]
    x, g, others = advance(
        sums[...],
        (own[:, :M], own[:, M : 2 * M], own[:, 2 * M :]),
        [others[:, start : start + size] for start, size in zip(offsets, WIDTHS)],
        mate[...],
        near[...],
        far[...],
        statics,
        lift_rows,
        (mate_kernel, near_kernel.at[SIDE:], far_kernel.at[SIDE:]),
    )
    return x, g, others, statics


def advance_kernel(*refs):
    dual_hbm, outs, (dual_ref, sems) = refs[16], refs[17:23], refs[23:]
    piece = whole_copy(dual_hbm, dual_ref, sems)
    even = is_even()
    x, g, others, statics = advanced(refs[:16], piece)
    pick = picks(refs[10][...], even)
    pieces = [piece(k, k >= 2) for k in range(len(STARTS))]
    image, row = tail(g, others, statics, pick, even, pieces)
    emit(outs, x, g, image, row, others)


def last_advance_kernel(*refs):
    dual_hbm, (own_out, others_out, row_out), (dual_ref, sems) = refs[16], refs[17:20], refs[20:]
    piece = whole_copy(dual_hbm, dual_ref, sems, STARTS[:2])
    x, g, others, _ = advanced(refs[:16], piece)
    own_out[:, :M] = x
    own_out[:, M:] = g
    others_out[...] = jnp.concatenate([others[1], others[4], others[5]], axis=1)
    total = jnp.sum(jnp.sum(g * g, axis=1, keepdims=True), axis=0, keepdims=True)
    row_out[...] = jnp.broadcast_to(total, row_out.shape)


def last_tail_kernel(*refs):
    ids, count, own, others, mortar, mate_mortar, match, first, dual_hbm = refs[:9]
    row_out, dual_ref, sems = refs[9:]
    piece = whole_copy(dual_hbm, dual_ref, sems)
    even = is_even()
    statics = statics_of(ids, count, mortar, mate_mortar, first)
    pick = picks(match[...], even)
    others = [
        None,
        others[:, :CONTACT],
        None,
        None,
        others[:, CONTACT : CONTACT + BLK],
        others[:, CONTACT + BLK :],
    ]
    pieces = [piece(k, True) for k in range(len(STARTS))]
    _, row = tail(own[:, M:], others, statics, pick, even, pieces)
    row_out[...] = jnp.broadcast_to(row, row_out.shape)


def finish_kernel(sums, own, x_out, norm_out):
    rows = sums[...]
    _, step = step_of(rows)
    x, _ = all_moved(own[:, :M], step, own[:, M : 2 * M])
    x_out[...] = x
    total = jnp.sum(rows, axis=0, keepdims=True)[:, 2 * CASES : 2 * CASES + 1]
    norm_out[...] = jnp.broadcast_to(jnp.sqrt(total), norm_out.shape)


VMEM_SPEC = pl.BlockSpec(memory_space=pltpu.VMEM)
SMEM_SPEC = pl.BlockSpec(memory_space=pltpu.SMEM)
HBM_SPEC = pl.BlockSpec(memory_space=pltpu.HBM)


WHOLE = [pltpu.VMEM((M, M), bf16), pltpu.SemaphoreType.DMA((len(STARTS),))]
BLOCK = [pltpu.VMEM((CONTACT, CONTACT), bf16), pltpu.SemaphoreType.DMA]


def call(kernel, specs, shapes, operands, scratch=WHOLE, grant=50):
    return pl.pallas_call(
        kernel,
        in_specs=specs,
        out_specs=[VMEM_SPEC] * len(shapes),
        out_shape=[jax.ShapeDtypeStruct(shape, kind) for shape, kind in shapes],
        scratch_shapes=scratch,
        compiler_params=pltpu.CompilerParams(vmem_limit_bytes=grant << 20),
    )(*operands)


def swapped(value, other):
    devices = lax.axis_size("sub")
    return lax.ppermute(value, "sub", [(i, other(i) % devices) for i in range(devices)])


def with_mate(value):
    half_axis = lax.axis_size("sub") // 2
    return swapped(value, lambda i: i + half_axis)


def with_near(value):
    return swapped(value, lambda i: i ^ 1)


def with_far(value):
    return swapped(value, lambda i: i + 1 if i % 2 else i - 1)


def with_case(value, bit):
    cases = lax.axis_size("case")
    return lax.ppermute(value, "case", [(i, i ^ bit) for i in range(cases)])


def spread_sums(copies, axis):
    devices = lax.axis_size(axis)
    rows = lax.all_to_all(copies.reshape(devices, 1, BLK), axis, 0, 0)
    return rows.reshape(devices, BLK)


def on_device(multipliers, right_side, dual_ops, glue_match, mortar, contact_ids, contact_count):
    devices = lax.axis_size("sub")
    mortar = mortar.reshape(CONTACT, BLK)
    match = glue_match[0]
    scalars = [SMEM_SPEC, SMEM_SPEC]

    mate_mortar = with_mate(mortar)
    q, first, to_near, to_far = call(
        prepare_kernel,
        scalars + [VMEM_SPEC] * 2 + [HBM_SPEC],
        [
            ((CASES, M), f32),
            ((3 * CASES, CONTACT), bf16),
            ((SIDE + CONTACT, BLK), bf16),
            ((SIDE + CONTACT, BLK), bf16),
        ],
        (contact_ids, contact_count, multipliers, right_side, dual_ops),
        grant=PREPARE_GRANT,
    )
    first, dual_later = lax.optimization_barrier((first, dual_ops))
    first = with_mate(first)
    near = near_kernel = with_near(to_near)
    far = far_kernel = with_far(to_far)
    (half,) = call(pack_kernel, [HBM_SPEC], [((HALF, CONTACT), bf16)], (dual_later,), scratch=BLOCK)
    half = with_mate(half)

    shapes = [
        ((CASES, 3 * M), f32),
        ((CASES, sum(WIDTHS)), f32),
        ((devices, BLK), f32),
        ((CASES, CONTACT), f32),
        ((CASES, BLK + CONTACT), f32),
        ((CASES, BLK + CONTACT), f32),
    ]
    own, others, copies, to_mate, to_near, to_far = call(
        begin_kernel,
        scalars + [VMEM_SPEC] * 8 + [HBM_SPEC],
        shapes,
        (
            contact_ids, contact_count, multipliers, q, first, near, far, mortar, mate_mortar,
            match, dual_ops,
        ),
    )
    for iteration in range(1, ITERS):
        sums = spread_sums(copies, "sub")
        mate = with_mate(to_mate)
        far = with_far(to_far)
        near = with_near(to_near)
        if iteration == 1:
            other_half = with_case(half, 1)
        operands = (
            contact_ids, contact_count, sums, own, others, mate, near, far, mortar,
            mate_mortar, match, first, near_kernel, far_kernel, half, other_half, dual_ops,
        )
        if iteration < ITERS - 1:
            own, others, copies, to_mate, to_near, to_far = call(
                advance_kernel,
                scalars + [VMEM_SPEC] * 14 + [HBM_SPEC],
                shapes,
                operands,
            )
    cases = lax.axis_size("case")
    own, others, norms = call(
        last_advance_kernel,
        scalars + [VMEM_SPEC] * 14 + [HBM_SPEC],
        [
            ((CASES, 2 * M), f32),
            ((CASES, CONTACT + 2 * BLK), f32),
            ((cases, BLK), f32),
        ],
        operands,
    )
    norms = spread_sums(norms, "case")
    (copies,) = call(
        last_tail_kernel,
        scalars + [VMEM_SPEC] * 6 + [HBM_SPEC],
        [((devices, BLK), f32)],
        (
            contact_ids, contact_count, own, others, mortar, mate_mortar, match, first,
            dual_ops,
        ),
    )
    lane = lax.broadcasted_iota(jnp.int32, (1, BLK), 1)
    norm_row = jnp.where(lane == 2 * CASES, jnp.sum(norms, axis=0, keepdims=True), 0.0)
    sums = spread_sums(copies + norm_row, "sub")
    x, norm = call(
        finish_kernel,
        [VMEM_SPEC, VMEM_SPEC],
        [((CASES, M), f32), ((1, BLK), f32)],
        (sums, own),
        scratch=[],
        grant=16,
    )
    return (x, norm[0, :1])


PREPARE_GRANT = 60


def solution(mesh):
    in_specs = (
        P("case", "sub"),
        P("case", "sub"),
        P("sub", None),
        P("sub", None, None),
        P("sub", None, None, None),
        P("sub", None),
        P("sub"),
    )
    out_specs = (P("case", "sub"), P())
    return jax.shard_map(
        on_device, mesh=mesh, in_specs=in_specs, out_specs=out_specs, check_vma=False
    )
```
